512 devices in a mesh: blk: 128 (over z, x, core), grp: 4 (over y).
Axes of the slice: x: 4, y: 4, z: 16, core: 2. Of those that a mesh axis runs over, the one named last changes fastest.
Arguments:
- checkpoint: bfloat16 [131072, 320], P(('blk', 'grp')), may hold values from -4 to 4
- adjoint_rhs: bfloat16 [131072, 320], P(('blk', 'grp')), may hold values from -6 to 6
- new_position: int32 [131072], P(('blk', 'grp')), may hold values from 0 to 131071, as said below
- old_position: int32 [131072], P(('blk', 'grp')), may hold values from 0 to 131071, as said below
- left_matrix: bfloat16 [320, 320], replicated, may hold values from -0.3125 to 0.3125
- right_matrix: bfloat16 [320, 320], replicated, may hold values from -0.3125 to 0.3125
- face_block: int32 [6, 131072], P(None, ('blk', 'grp')), may hold values from -1 to 131071, as said below
- face_weight: float32 [6, 131072], P(None, ('blk', 'grp')), may hold values from 0.3 to 0.9
- donor_block: int32 [2, 131072], P(None, ('blk', 'grp')), may hold values from 0 to 131071, as said below
- donor_weight: float32 [2, 131072], P(None, ('blk', 'grp')), may hold values from 0.2 to 0.7
Outputs:
- adjoint: float32 [131072, 320], P(('blk', 'grp'))
The draws below stay inside these ranges and needn't reach their ends.
Inputs may be any that keep to these rules, and one draw needn't show every extreme that they name: `new_position`: A permutation of the block indices that keeps each block's index along grp; the blocks of one device go to 64 devices along blk, exactly 4 blocks to each of them. `old_position`: the inverse permutation of new_position. `face_block`: each entry is -1 or a block of the same grp index whose place in that group's order of blocks (blk index times 256 plus the local index) lies within 256 places of the block's own, taken cyclically. `donor_block`: each donor lies on the device of the same blk index and another grp index, among the first 128 blocks of that device in the new order.
All inputs are finite; a program needn't handle non-finite values.
Results may differ from the reference program's by a relative error of at most 0.0014.
Values may be sent and summed in bfloat16 or wider, within the bound.
A program may use at most 64 MiB of HBM per device.

```python
import jax
import jax.numpy as jnp
from jax import lax

BLOCK_VALUES = 320
FACES = 6
DONORS = 2
SWEEPS = 2
BLK_DEV = 256
CAP = 4
DONOR_ROWS = 128
NBLOCKS = 131072
N_BLK = 128
N_GRP = 4


def migration_tables(key):
    base_key = jax.random.fold_in(key, 7)
    shift_key, perm_key = jax.random.split(base_key)
    total_blocks = BLK_DEV * N_BLK * N_GRP
    shift_ids = jnp.arange(N_BLK, dtype=jnp.int32)
    scores = jax.random.permutation(shift_key, N_BLK).astype(jnp.int32)
    scores = jnp.where(shift_ids == N_BLK // 2, -2, jnp.where(shift_ids == 1, -1, scores))
    shifts = jnp.argsort(scores, stable=True).astype(jnp.int32)[:BLK_DEV // CAP]
    row_keys = jax.random.split(perm_key, N_BLK * N_GRP)
    local_perms = jax.vmap(lambda one_key: jax.random.permutation(one_key, BLK_DEV))(row_keys)
    global_ids = jnp.arange(total_blocks, dtype=jnp.int32)
    device_ids = global_ids // BLK_DEV
    blk_ids = device_ids // N_GRP
    grp_ids = device_ids % N_GRP
    local_ids = global_ids % BLK_DEV
    target_blk = (blk_ids + shifts[local_ids // CAP]) % N_BLK
    target_local = local_perms[target_blk * N_GRP + grp_ids, local_ids]
    new_ids = ((target_blk * N_GRP + grp_ids) * BLK_DEV + target_local).astype(jnp.int32)
    old_ids = jnp.zeros((total_blocks,), jnp.int32).at[new_ids].set(global_ids)
    return (new_ids, old_ids)


def draw_new_position(key, part):
    return migration_tables(key)[0]


def draw_old_position(key, part):
    return migration_tables(key)[1]


def draw_face_block(key, part):
    off_key, wall_key = jax.random.split(jax.random.fold_in(key, 13))
    total_blocks = BLK_DEV * N_BLK * N_GRP
    global_ids = jnp.arange(total_blocks, dtype=jnp.int32)
    device_ids = global_ids // BLK_DEV
    blk_ids = device_ids // N_GRP
    grp_ids = device_ids % N_GRP
    local_ids = global_ids % BLK_DEV
    chain = blk_ids * BLK_DEV + local_ids
    chain_len = N_BLK * BLK_DEV
    offsets = jax.random.randint(off_key, (6, total_blocks), -BLK_DEV, BLK_DEV + 1)
    moved = (chain[None, :] + offsets) % chain_len
    neighbour = (moved // BLK_DEV * N_GRP + grp_ids[None, :]) * BLK_DEV + moved % BLK_DEV
    walls = jax.random.randint(wall_key, (6, total_blocks), 0, 6) == 0
    return jnp.where(walls, -1, neighbour).astype(jnp.int32)


def draw_donor_block(key, part):
    grp_key, local_key = jax.random.split(jax.random.fold_in(key, 17))
    total_blocks = BLK_DEV * N_BLK * N_GRP
    global_ids = jnp.arange(total_blocks, dtype=jnp.int32)
    device_ids = global_ids // BLK_DEV
    blk_ids = device_ids // N_GRP
    grp_ids = device_ids % N_GRP
    other_grp = (grp_ids[None, :] + jax.random.randint(grp_key, (2, total_blocks), 1, N_GRP)) % N_GRP
    donor_local = jax.random.randint(local_key, (2, total_blocks), 0, DONOR_ROWS)
    return ((blk_ids[None, :] * N_GRP + other_grp) * BLK_DEV + donor_local).astype(jnp.int32)


def block_scale(key, extent, cuts, least, top_value):
    def one(dim, shards_of):
        steps = jax.random.uniform(jax.random.fold_in(jax.random.fold_in(key, 6), dim), (shards_of,), jnp.float32, least / len(cuts), top_value / len(cuts))
        return jnp.repeat(jnp.exp(steps), extent[dim] // shards_of).reshape((-1,) + (1,) * (len(extent) - dim - 1))

    level = one(*cuts[0])
    for cut in cuts[1:]:
        level = level * one(*cut)
    return level


def bell_draw(rng, extent, spread, most, cuts=(), kind=jnp.bfloat16):
    values = spread * jax.random.normal(rng, extent, jnp.float32)
    if cuts:
        values = values * block_scale(rng, extent, cuts, -0.22, 0.18)
    return jnp.clip(values, -most, most).astype(kind)


def setup_inputs(seed: int = 0) -> dict:
    key_list = jax.random.split(jax.random.key(seed), 11)
    return {
        "checkpoint": bell_draw(key_list[0], (NBLOCKS, BLOCK_VALUES), 1.0, 4.0, ((0, 512),)),
        "adjoint_rhs": bell_draw(key_list[1], (NBLOCKS, BLOCK_VALUES), 1.0, 6.0, ((0, 512),)),
        "new_position": draw_new_position(jax.random.fold_in(key_list[10], 71), 0),
        "old_position": draw_old_position(jax.random.fold_in(key_list[10], 71), 0),
        "left_matrix": bell_draw(key_list[4], (BLOCK_VALUES, BLOCK_VALUES), BLOCK_VALUES ** -0.5, 0.3125),
        "right_matrix": bell_draw(key_list[5], (BLOCK_VALUES, BLOCK_VALUES), BLOCK_VALUES ** -0.5, 0.3125),
        "face_block": draw_face_block(jax.random.fold_in(key_list[10], 71), 0),
        "face_weight": jnp.clip(0.3 + 0.59999996 * jax.random.uniform(key_list[7], (FACES, NBLOCKS), jnp.float32) ** block_scale(key_list[7], (FACES, NBLOCKS), ((1, 512),), -0.2, 0.2), 0.3, 0.9),
        "donor_block": draw_donor_block(jax.random.fold_in(key_list[10], 71), 0),
        "donor_weight": jnp.clip(0.2 + 0.5 * jax.random.uniform(key_list[9], (DONORS, NBLOCKS), jnp.float32) ** block_scale(key_list[9], (DONORS, NBLOCKS), ((1, 512),), -0.2, 0.2), 0.2, 0.7),
    }


def coefficients(state):
    values = state.astype(jnp.float32)
    left_gain = 0.5 * jnp.tanh(values)
    right_gain = 0.4 * jnp.tanh(1.5 * values - 0.5)
    dual_diag = 2.0 + values * values
    return left_gain, right_gain, dual_diag


def transposed_apply(adjoint, left_gain, right_gain, left_matrix, right_matrix, left_trans, right_trans):
    rounded = adjoint.astype(jnp.bfloat16)
    first_proj = jnp.dot(rounded, left_matrix, preferred_element_type=jnp.float32)
    second_proj = jnp.dot(rounded, right_trans, preferred_element_type=jnp.float32)
    first_mid = (first_proj * left_gain).astype(jnp.bfloat16)
    second_mid = (second_proj * right_gain).astype(jnp.bfloat16)
    return jnp.dot(first_mid, right_matrix, preferred_element_type=jnp.float32) + jnp.dot(second_mid, left_trans, preferred_element_type=jnp.float32)


def face_sum(block_pool, face_index, face_valid, face_weight):
    row_count = face_index.shape[1]
    total_face = jnp.zeros((row_count, block_pool.shape[1]), jnp.float32)
    for face_id in range(face_index.shape[0]):
        fetched = jnp.take(block_pool, face_index[face_id], axis=0).reshape(row_count, 5, 4, 4, 4)
        cell_axis = 2 + face_id // 2
        from_cell = 3 if face_id % 2 == 0 else 0
        face_slab = lax.slice_in_dim(fetched, from_cell, from_cell + 1, axis=cell_axis)
        scale_face = jnp.where(face_valid[face_id], face_weight[face_id], 0.0)
        face_slab = face_slab * scale_face.reshape(row_count, 1, 1, 1, 1)
        pad_shape = list(face_slab.shape)
        pad_shape[cell_axis] = 3
        padding = jnp.zeros(pad_shape, jnp.float32)
        if face_id % 2 == 0:
            placed = jnp.concatenate([face_slab, padding], axis=cell_axis)
        else:
            placed = jnp.concatenate([padding, face_slab], axis=cell_axis)
        total_face = total_face + placed.reshape(row_count, block_pool.shape[1])
    return total_face


def fringe_sum(block_pool, donor_index, donor_weight):
    total_fringe = jnp.zeros((donor_index.shape[1], block_pool.shape[1]), jnp.float32)
    for donor_id in range(donor_index.shape[0]):
        fetched = jnp.take(block_pool, donor_index[donor_id], axis=0)
        total_fringe = total_fringe + donor_weight[donor_id][:, None] * fetched
    return total_fringe


def reference(checkpoint, adjoint_rhs, new_position, old_position, left_matrix, right_matrix, face_block, face_weight, donor_block, donor_weight):
    state = jnp.zeros_like(checkpoint).at[new_position].set(checkpoint)
    rhs_float = adjoint_rhs[old_position].astype(jnp.float32)
    left_gain, right_gain, dual_diag = coefficients(state)
    left_trans = left_matrix.T
    right_trans = right_matrix.T
    face_valid = face_block >= 0
    face_index = jnp.where(face_valid, face_block, 0).astype(jnp.int32)
    result = rhs_float / dual_diag
    for sweep_step in range(SWEEPS):
        applied = transposed_apply(result, left_gain, right_gain, left_matrix, right_matrix, left_trans, right_trans)
        face_term = face_sum(result, face_index, face_valid, face_weight)
        fringe_term = fringe_sum(result, donor_block, donor_weight)
        result = (((rhs_float - applied) - face_term) - fringe_term) / dual_diag
    return result
```

```python
import jax
import jax.numpy as jnp
from jax import lax
from jax.experimental import pallas as pl
from jax.experimental.pallas import tpu as pltpu
from jax.sharding import PartitionSpec as P

MESH = pl.DeviceIdType.MESH
ROWS = 256
VALS = 320
PADDED = 384
PACKED = 640
BLK = 128
GRP = 4
NZ = 16
ND = 8
CAP = 4
SLOTS = BLK * CAP
DONORS = 128
CHUNKS = 4
CHUNK = SLOTS // CHUNKS
F32 = jnp.float32
BF16 = jnp.bfloat16
ORDER = (8, 9, 7, 10, 6, 11, 5, 12, 4, 13, 3, 14, 2, 15, 1, 0)


def dot(a, b):
    return jnp.dot(a, b, preferred_element_type=F32)


def iota(shape, dim):
    return lax.broadcasted_iota(jnp.int32, shape, dim)


def piece_of(blk, me):
    away = (blk // ND - me // ND) & (NZ - 1)
    place = jnp.where(away == 0, NZ - 1, jnp.where(away <= NZ // 2, NZ - 2 * away, 2 * away - NZ - 1))
    return place, (blk - me) & (ND - 1)


def kernel(
    ckpt, rhs, npos, opos, lmat, rmat, fblk, fw, dblk, dw, out,
    send, zrecv, zpack, got, table, onehot, donor_hot, pool, donor_pool, mats_a, mats_b,
    left_gain, right_gain, inv_diag, rhs_f, value,
    zs_sem, zr_sem, ds_sem, dr_sem, hs_sem, hr_sem,
):
    me = lax.axis_index("blk")
    grp = lax.axis_index("grp")
    my_z, my_d = me // ND, me % ND
    below, above = (me + BLK - 1) % BLK, (me + 1) % BLK

    barrier = pltpu.get_barrier_semaphore()

    def greet(**where):
        pl.semaphore_signal(barrier, inc=1, device_id=where, device_id_type=MESH)

    for away in ORDER[:-1]:
        greet(blk=(my_z + away) % NZ * ND + my_d)
    for e in range(1, ND):
        greet(blk=my_z * ND + (my_d + e) % ND)
    for g in range(1, GRP):
        greet(grp=(grp + g) % GRP)
    greet(blk=below)
    greet(blk=above)

    target = npos[...] >> 10
    place, e = piece_of(target, me)
    key = place * ND + (((target & (ND - 1)) - my_d) & (ND - 1))
    hot = (key == iota((BLK, ROWS), 0)).astype(BF16)
    before = (iota((ROWS, ROWS), 0) < iota((ROWS, ROWS), 1)).astype(BF16)
    rank = jnp.sum(hot.astype(F32) * dot(hot, before), axis=0, keepdims=True)
    slot = (key * CAP).astype(F32) + rank
    put = (slot == iota((SLOTS, ROWS), 0).astype(F32)).astype(BF16)
    tail = jnp.concatenate([ckpt[:, 256:VALS], rhs[:, 256:VALS]], axis=1)
    send[:, 0:256] = dot(put, ckpt[:, 0:256]).astype(BF16)
    send[:, 256:512] = dot(put, rhs[:, 0:256]).astype(BF16)
    send[:, 512:640] = dot(put, tail).astype(BF16)

    pl.semaphore_wait(barrier, NZ - 1 + ND - 1 + GRP - 1 + 2)

    piece = ND * CAP
    z_copies = []
    for p, away in enumerate(ORDER[:-1]):
        rows = pl.ds(p * piece, piece)
        z_copies.append(
            pltpu.make_async_remote_copy(
                src_ref=send.at[rows],
                dst_ref=zrecv.at[rows],
                send_sem=zs_sem.at[p],
                recv_sem=zr_sem.at[p],
                device_id={"blk": (my_z + away) % NZ * ND + my_d},
                device_id_type=MESH,
            )
        )
        z_copies[-1].start()
    own = pl.ds((NZ - 1) * piece, piece)
    zrecv[own, :] = send[own, :]

    table[...] = jnp.zeros_like(table)
    faces = fblk[...]
    face_place = (((faces >> 10) - me + 1) & (BLK - 1)) * ROWS + (faces & (ROWS - 1))
    table[0:6, :] = jnp.where(faces >= 0, face_place, -1).astype(F32)
    table[8:14, :] = fw[...]
    donors = dblk[...]
    donor_place = ((((donors >> 8) - grp) & (GRP - 1)) - 1) * DONORS + (donors & (ROWS - 1))
    table[16:18, :] = donor_place.astype(F32)
    table[24:26, :] = dw[...]
    anchor = opos[...] >> 10
    place, e = piece_of(anchor, me)
    e = (my_d - (anchor & (ND - 1))) & (ND - 1)
    away = (my_z - anchor // ND) & (NZ - 1)
    place = jnp.where(away == 0, NZ - 1, jnp.where(away <= NZ // 2, NZ - 2 * away, 2 * away - NZ - 1))
    order_row = ((place * ND + e) * ROWS + (opos[...] & (ROWS - 1))).astype(F32)
    base = (place >> 2) * CHUNK + e * 16 + (place & 3) * CAP
    table[32:33, :] = order_row
    table[40:41, :] = base.astype(F32)
    columns = jnp.transpose(table[...])

    def column(n):
        return columns[:, n : n + 1]

    smaller = (order_row < column(32)).astype(BF16)
    rank = dot(smaller, jnp.ones((ROWS, 128), BF16)).astype(jnp.int32) & (CAP - 1)
    recv_slot = rank.astype(F32) + column(40)
    lanes = iota((ROWS, 128), 1).astype(F32)
    pick = jnp.concatenate(
        [(recv_slot == lanes + 128.0 * t).astype(BF16) for t in range(SLOTS // 128)], axis=1
    )
    pool_lane = iota((ROWS, 3 * ROWS), 1).astype(F32)
    for f in range(6):
        onehot[f * ROWS : (f + 1) * ROWS, :] = (column(f) == pool_lane).astype(BF16)
    donor_lane = iota((ROWS, 3 * DONORS), 1).astype(F32)
    for k in range(2):
        donor_hot[k * ROWS : (k + 1) * ROWS, :] = (column(16 + k) == donor_lane).astype(BF16)

    mats_a[...] = jnp.zeros_like(mats_a)
    mats_b[...] = jnp.zeros_like(mats_b)
    mats_a[0:VALS, 0:VALS] = lmat[...]
    mats_b[0:VALS, 0:VALS] = rmat[...]
    mats_a[:, PADDED:] = jnp.transpose(mats_b[0:PADDED, :])
    mats_b[PADDED:, :] = jnp.transpose(mats_a[:, 0:PADDED])

    row, col = iota((CHUNK, CHUNK), 0), iota((CHUNK, CHUNK), 1)
    regroup = (col == ((row >> 2) & 3) * piece + (row >> 4) * CAP + (row & 3)).astype(BF16)
    d_copies = []
    per = CHUNK // ND
    for q in range(CHUNKS):
        for p in range(4 * q, min(4 * q + 4, NZ - 1)):
            z_copies[p].wait_recv()
        rows = slice(q * CHUNK, (q + 1) * CHUNK)
        moved = dot(regroup, zrecv[rows, :]).astype(BF16)
        zpack[rows, :] = moved
        for e in range(1, ND):
            part = pl.ds(q * CHUNK + e * per, per)
            d_copies.append(
                pltpu.make_async_remote_copy(
                    src_ref=zpack.at[part],
                    dst_ref=got.at[part],
                    send_sem=ds_sem.at[q * (ND - 1) + e - 1],
                    recv_sem=dr_sem.at[q * (ND - 1) + e - 1],
                    device_id={"blk": my_z * ND + (my_d + e) % ND},
                    device_id_type=MESH,
                )
            )
            d_copies[-1].start()
        got[q * CHUNK : q * CHUNK + per, :] = moved[0:per, :]
    for copy in d_copies:
        copy.wait_recv()

    valid = iota((ROWS, 128), 1) < 64
    last = dot(pick, got[:, 512:640])
    state = jnp.concatenate([dot(pick, got[:, 0:256]), jnp.where(valid, last, 0.0)], axis=1)
    diag = 1.0 / (2.0 + state * state)
    inv_diag[...] = diag
    rhs_new = jnp.concatenate(
        [dot(pick, got[:, 256:512]), jnp.where(valid, pltpu.roll(last, 64, 1), 0.0)], axis=1
    )
    rhs_f[...] = rhs_new
    first = rhs_new * diag
    value[...] = first
    left_gain[...] = 0.5 * jnp.tanh(state)
    right_gain[...] = 0.4 * jnp.tanh(1.5 * state - 0.5)

    lane = iota((ROWS, 128), 1)

    def sweep(s, carry):
        rounded = value[...].astype(BF16)
        pool[s, ROWS : 2 * ROWS, :] = rounded
        copies = []
        for n, (where, dst) in enumerate(((above, 0), (below, 2 * ROWS))):
            copies.append(
                pltpu.make_async_remote_copy(
                    src_ref=pool.at[s, pl.ds(ROWS, ROWS)],
                    dst_ref=pool.at[s, pl.ds(dst, ROWS)],
                    send_sem=hs_sem.at[s, n],
                    recv_sem=hr_sem.at[s, n],
                    device_id={"blk": where},
                    device_id_type=MESH,
                )
            )
        for g in range(1, GRP):
            copies.append(
                pltpu.make_async_remote_copy(
                    src_ref=pool.at[s, pl.ds(ROWS, DONORS)],
                    dst_ref=donor_pool.at[s, pl.ds((g - 1) * DONORS, DONORS)],
                    send_sem=hs_sem.at[s, 1 + g],
                    recv_sem=hr_sem.at[s, 1 + g],
                    device_id={"grp": (grp + GRP - g) % GRP},
                    device_id_type=MESH,
                )
            )
        for copy in copies:
            copy.start()

        proj = dot(rounded, mats_a[...])
        mid_l = (proj[:, 0:PADDED] * left_gain[...]).astype(BF16)
        mid_r = (proj[:, PADDED:] * right_gain[...]).astype(BF16)
        applied = dot(mid_l, mats_b[0:PADDED, :]) + dot(mid_r, mats_b[PADDED:, :])
        value[...] = rhs_f[...] - applied

        for copy in copies:
            copy.wait_recv()
        tiles = [jnp.zeros((ROWS, 128), F32) for _ in range(3)]
        for f in range(6):
            stride = (16, 4, 1)[f // 2]
            cell = lane // stride % 4
            fetched = dot(onehot[f * ROWS : (f + 1) * ROWS, :], pool[s]) * table_t(f)
            for t in range(3):
                tile = fetched[:, 128 * t : 128 * t + 128]
                if f % 2 == 0:
                    moved = jnp.where(cell == 0, pltpu.roll(tile, 128 - 3 * stride, 1), 0.0)
                else:
                    moved = jnp.where(cell == 3, pltpu.roll(tile, 3 * stride, 1), 0.0)
                tiles[t] = tiles[t] + moved
        total = jnp.concatenate(tiles, axis=1)
        donor = dot(donor_hot[...], donor_pool[s])
        fringe = donor[0:ROWS] * column(24) + donor[ROWS:] * column(25)
        value[...] = ((value[...] - total) - fringe) * inv_diag[...]
        for copy in copies:
            copy.wait_send()
        return carry

    def table_t(f):
        return column(8 + f)

    lax.fori_loop(0, 2, sweep, 0)
    out[...] = value[:, 0:VALS]
    for copy in z_copies + d_copies:
        copy.wait_send()


def body(ckpt, rhs, npos, opos, lmat, rmat, fblk, fw, dblk, dw):
    vmem = pl.BlockSpec(memory_space=pltpu.VMEM)
    dma = pltpu.SemaphoreType.DMA
    return pl.pallas_call(
        kernel,
        out_shape=jax.ShapeDtypeStruct((ROWS, VALS), F32),
        in_specs=[vmem] * 10,
        out_specs=vmem,
        scratch_shapes=[
            pltpu.VMEM((SLOTS, PACKED), BF16),
            pltpu.VMEM((SLOTS, PACKED), BF16),
            pltpu.VMEM((SLOTS, PACKED), BF16),
            pltpu.VMEM((SLOTS, PACKED), BF16),
            pltpu.VMEM((128, ROWS), F32),
            pltpu.VMEM((6 * ROWS, 3 * ROWS), BF16),
            pltpu.VMEM((2 * ROWS, 3 * DONORS), BF16),
            pltpu.VMEM((2, 3 * ROWS, PADDED), BF16),
            pltpu.VMEM((2, 3 * DONORS, PADDED), BF16),
            pltpu.VMEM((PADDED, 2 * PADDED), BF16),
            pltpu.VMEM((2 * PADDED, PADDED), BF16),
        ]
        + [pltpu.VMEM((ROWS, PADDED), F32)] * 5
        + [
            dma((NZ - 1,)), dma((NZ - 1,)),
            dma((CHUNKS * (ND - 1),)), dma((CHUNKS * (ND - 1),)),
            dma((2, 5)), dma((2, 5)),
        ],
        compiler_params=pltpu.CompilerParams(collective_id=0, has_side_effects=True),
    )(ckpt, rhs, npos.reshape(1, ROWS), opos.reshape(1, ROWS), lmat, rmat, fblk, fw, dblk, dw)


def solution(mesh):
    row, vec, many = P(("blk", "grp"), None), P(("blk", "grp")), P(None, ("blk", "grp"))
    return jax.shard_map(
        body,
        mesh=mesh,
        in_specs=(row, row, vec, vec, P(), P(), many, many, many, many),
        out_specs=row,
        check_vma=False,
    )
```

```python
import jax
import jax.numpy as jnp
from jax import lax
from jax.experimental import pallas as pl
from jax.experimental.pallas import tpu as pltpu
from jax.sharding import PartitionSpec as P

MESH = pl.DeviceIdType.MESH
ROWS = 256
VALS = 320
MAIN = 256
PADDED = 384
PACKED = 640
BLK = 128
GRP = 4
NZ = 16
ND = 8
CAP = 4
SLOTS = BLK * CAP
DONORS = 128
PER_CHUNK = 2
CHUNKS = NZ // PER_CHUNK
CHUNK = SLOTS // CHUNKS
PIECE = ND * CAP
PART = PER_CHUNK * CAP
F32 = jnp.float32
BF16 = jnp.bfloat16
ORDER = (0, 1, 15, 8, 9, 7, 10, 6, 11, 5, 12, 4, 13, 3, 14, 2)


def dot(a, b):
    return jnp.dot(a, b, preferred_element_type=F32)


def dot_t(a, b):
    return lax.dot_general(a, b, (((1,), (1,)), ((), ())), preferred_element_type=F32)


def iota(shape, dim):
    return lax.broadcasted_iota(jnp.int32, shape, dim)


def place_of(away):
    away = away & (NZ - 1)
    far = jnp.where(away <= NZ // 2, NZ + 3 - 2 * away, 2 * away - NZ + 2)
    return jnp.where(away <= 1, away, jnp.where(away == NZ - 1, 2, far))


def remote(src, dst, send_sem, recv_sem, **where):
    return pltpu.make_async_remote_copy(
        src_ref=src, dst_ref=dst, send_sem=send_sem, recv_sem=recv_sem, device_id=where, device_id_type=MESH
    )


def kernel(
    ckpt_hbm, rhs_hbm, npos_hbm, opos_hbm, lmat_hbm, rmat_hbm, fblk_hbm, fw_hbm, dblk_hbm, dw_hbm, out,
    ckpt, rhs, npos, opos, lmat, rmat, fblk, fw, dblk, dw,
    send, zrecv, zpack, got, table, onehot, donor_hot,
    pool, pool_tail, own_tail, halo_tail, donor_pool, donor_tail, donor_in, mats_a, mats_b,
    left_gain, right_gain, inv_diag, rhs_f, value,
    in_sem, zs_sem, zr_sem, ds_sem, dr_sem, hs_sem, hr_sem,
):
    me = lax.axis_index("blk")
    grp = lax.axis_index("grp")
    my_z, my_d = me // ND, me % ND
    below, above = (me + BLK - 1) % BLK, (me + 1) % BLK

    barrier = pltpu.get_barrier_semaphore()

    def greet(**where):
        pl.semaphore_signal(barrier, inc=1, device_id=where, device_id_type=MESH)

    for away in (8, 7, 9, 6, 10, 5, 11, 4, 12, 3, 13, 2, 14, 1, 15):
        greet(blk=(my_z + away) % NZ * ND + my_d)
    for e in range(1, ND):
        greet(blk=my_z * ND + (my_d + e) % ND)
    for g in range(1, GRP):
        greet(grp=(grp + g) % GRP)
    greet(blk=below)
    greet(blk=above)

    pairs = (
        (npos_hbm, npos), (ckpt_hbm, ckpt), (rhs_hbm, rhs), (opos_hbm, opos), (fblk_hbm, fblk),
        (fw_hbm, fw), (dblk_hbm, dblk), (dw_hbm, dw), (lmat_hbm, lmat), (rmat_hbm, rmat),
    )
    loads = [pltpu.make_async_copy(a, b, in_sem.at[i]) for i, (a, b) in enumerate(pairs)]
    for load in loads:
        load.start()

    loads[0].wait()
    target = npos[...] >> 10
    key = place_of((target >> 3) - my_z) * ND + (((target & (ND - 1)) - my_d) & (ND - 1))
    hot = (key == iota((BLK, ROWS), 0)).astype(BF16)
    earlier = (iota((ROWS, ROWS), 0) < iota((ROWS, ROWS), 1)).astype(BF16)
    rank = jnp.sum(hot.astype(F32) * dot(hot, earlier), axis=0, keepdims=True)
    slot = (key * CAP).astype(F32) + rank
    put = (slot == iota((SLOTS, ROWS), 0).astype(F32)).astype(BF16)
    loads[1].wait()
    loads[2].wait()
    tail = jnp.concatenate([ckpt[MAIN:VALS, :], rhs[MAIN:VALS, :]], axis=0)
    send[:, 0:256] = dot_t(put, ckpt[0:MAIN, :]).astype(BF16)
    send[:, 256:512] = dot_t(put, rhs[0:MAIN, :]).astype(BF16)
    send[:, 512:640] = dot_t(put, tail).astype(BF16)

    pl.semaphore_wait(barrier, NZ - 1 + ND - 1 + GRP - 1 + 2)

    z_copies = [None]
    for p in range(1, NZ):
        rows = pl.ds(p * PIECE, PIECE)
        z_copies.append(
            remote(
                send.at[rows], zrecv.at[rows], zs_sem.at[p - 1], zr_sem.at[p - 1],
                blk=(my_z + ORDER[p]) % NZ * ND + my_d,
            )
        )
        z_copies[-1].start()
    zrecv[0:PIECE, :] = send[0:PIECE, :]

    row, col = iota((CHUNK, CHUNK), 0), iota((CHUNK, CHUNK), 1)
    regroup = (col == ((row // CAP) % PER_CHUNK) * PIECE + (row // PART) * CAP + row % CAP).astype(BF16)
    d_copies = []

    def pass_on(q):
        for p in range(PER_CHUNK * q, PER_CHUNK * (q + 1)):
            if p:
                z_copies[p].wait_recv()
        rows = slice(q * CHUNK, (q + 1) * CHUNK)
        moved = dot(regroup, zrecv[rows, :]).astype(BF16)
        zpack[rows, :] = moved
        for e in (4, 5, 3, 2, 6, 7, 1):
            part = pl.ds(q * CHUNK + e * PART, PART)
            n = q * (ND - 1) + e - 1
            d_copies.append(
                remote(
                    zpack.at[part], got.at[part], ds_sem.at[n], dr_sem.at[n],
                    blk=my_z * ND + (my_d + e) % ND,
                )
            )
            d_copies[-1].start()
        got[q * CHUNK : q * CHUNK + PART, :] = moved[0:PART, :]

    for load in loads[3:]:
        load.wait()
    table[...] = jnp.zeros_like(table)
    faces = fblk[...]
    face_place = (((faces >> 10) - me + 1) & (BLK - 1)) * ROWS + (faces & (ROWS - 1))
    table[0:6, :] = jnp.where(faces >= 0, face_place, -1).astype(F32)
    table[8:14, :] = fw[...]
    donors = dblk[...]
    donor_place = ((((donors >> 8) - grp) & (GRP - 1)) - 1) * DONORS + (donors & (ROWS - 1))
    table[16:18, :] = donor_place.astype(F32)
    table[24:26, :] = dw[...]
    anchor = opos[...] >> 10
    e = (my_d - (anchor & (ND - 1))) & (ND - 1)
    place = place_of(my_z - (anchor >> 3))
    order_row = ((place * ND + e) * ROWS + (opos[...] & (ROWS - 1))).astype(F32)
    base = (place // PER_CHUNK) * CHUNK + e * PART + (place % PER_CHUNK) * CAP
    table[32:33, :] = order_row
    table[40:41, :] = base.astype(F32)
    columns = jnp.transpose(table[...])

    def column(n):
        return columns[:, n : n + 1]

    smaller = (order_row < column(32)).astype(BF16)
    rank = dot(smaller, jnp.ones((ROWS, 128), BF16)).astype(jnp.int32) & (CAP - 1)
    recv_slot = rank.astype(F32) + column(40)
    lanes = iota((ROWS, 128), 1).astype(F32)
    pick = jnp.concatenate(
        [(recv_slot == lanes + 128.0 * t).astype(BF16) for t in range(SLOTS // 128)], axis=1
    )
    pool_lane = iota((ROWS, 3 * ROWS), 1).astype(F32)
    for f in range(6):
        onehot[f * ROWS : (f + 1) * ROWS, :] = (column(f) == pool_lane).astype(BF16)
    donor_lane = iota((ROWS, 3 * DONORS), 1).astype(F32)
    for k in range(2):
        donor_hot[k * ROWS : (k + 1) * ROWS, :] = (column(16 + k) == donor_lane).astype(BF16)

    mats_a[...] = jnp.zeros_like(mats_a)
    mats_b[...] = jnp.zeros_like(mats_b)
    mats_a[0:VALS, 0:VALS] = lmat[...]
    mats_b[0:VALS, 0:VALS] = rmat[...]
    mats_a[:, PADDED:] = jnp.transpose(mats_b[0:PADDED, :])
    mats_b[PADDED:, :] = jnp.transpose(mats_a[:, 0:PADDED])

    for q in range(CHUNKS):
        pass_on(q)
    for copy in d_copies:
        copy.wait_recv()

    half = iota((ROWS, 128), 1) < 64
    last = dot(pick, got[:, 512:640])
    state = jnp.concatenate([dot(pick, got[:, 0:256]), jnp.where(half, last, 0.0)], axis=1)
    diag = 1.0 / (2.0 + state * state)
    inv_diag[...] = diag
    rhs_new = jnp.concatenate(
        [dot(pick, got[:, 256:512]), jnp.where(half, pltpu.roll(last, 64, 1), 0.0)], axis=1
    )
    rhs_f[...] = rhs_new
    value[...] = rhs_new * diag

    def stage(s, h, rows):
        at = ROWS + DONORS * h
        pool[s, at : at + DONORS, :] = rows[:, 0:MAIN].astype(BF16)
        tails = rows[:, MAIN:]
        pool_tail[s, at : at + DONORS, :] = tails.astype(BF16)
        both = jnp.where(half[0:64], tails[0:64], pltpu.roll(tails[64:128], 64, 1))
        own_tail[s, 64 * h : 64 * h + 64, :] = both.astype(BF16)

    def send_donors(s):
        copies = []
        for g in (2, 1, 3):
            n = 4 + 2 * (g - 1)
            to = (grp + GRP - g) % GRP
            copies.append(
                remote(
                    pool.at[s, pl.ds(ROWS, DONORS)], donor_pool.at[s, pl.ds((g - 1) * DONORS, DONORS)],
                    hs_sem.at[s, n], hr_sem.at[s, n], grp=to,
                )
            )
            copies.append(
                remote(
                    own_tail.at[s, pl.ds(0, 64)], donor_in.at[s, pl.ds((g - 1) * 64, 64)],
                    hs_sem.at[s, n + 1], hr_sem.at[s, n + 1], grp=to,
                )
            )
        for copy in copies:
            copy.start()
        return copies

    def send_halo(s):
        copies = []
        for n, (to, dst) in enumerate(((above, 0), (below, 2))):
            copies.append(
                remote(
                    pool.at[s, pl.ds(ROWS, ROWS)], pool.at[s, pl.ds(dst * ROWS, ROWS)],
                    hs_sem.at[s, 2 * n], hr_sem.at[s, 2 * n], blk=to,
                )
            )
            copies.append(
                remote(
                    own_tail.at[s], halo_tail.at[s, n],
                    hs_sem.at[s, 2 * n + 1], hr_sem.at[s, 2 * n + 1], blk=to,
                )
            )
        for copy in copies:
            copy.start()
        return copies

    def spread(packed):
        wide = packed.astype(F32)
        return packed, pltpu.roll(wide, 64, 1).astype(BF16)

    stage(0, 0, value[0:DONORS, :])
    donor_copies = send_donors(0)
    stage(0, 1, value[DONORS:, :])
    halo_copies = send_halo(0)
    left_gain[...] = 0.5 * jnp.tanh(state)
    right_gain[...] = 0.4 * jnp.tanh(1.5 * state - 0.5)

    lane = iota((ROWS, 128), 1)
    for s in range(2):
        rounded = value[...].astype(BF16)
        proj = dot(rounded, mats_a[...])
        mid_l = (proj[:, 0:PADDED] * left_gain[...]).astype(BF16)
        mid_r = (proj[:, PADDED:] * right_gain[...]).astype(BF16)
        applied = dot(mid_l, mats_b[0:PADDED, :]) + dot(mid_r, mats_b[PADDED:, :])
        value[...] = rhs_f[...] - applied

        for copy in halo_copies:
            copy.wait_recv()
        for n, dst in enumerate((0, 2 * ROWS)):
            for h in range(2):
                even, odd = spread(halo_tail[s, n, 64 * h : 64 * h + 64, :])
                at = dst + DONORS * h
                pool_tail[s, at : at + 64, :] = even
                pool_tail[s, at + 64 : at + 128, :] = odd
        tiles = [jnp.zeros((ROWS, 128), F32) for _ in range(3)]
        for f in range(6):
            stride = (16, 4, 1)[f // 2]
            cell = lane // stride % 4
            hot = onehot[f * ROWS : (f + 1) * ROWS, :]
            weight = column(8 + f)
            fetched = dot(hot, pool[s]) * weight
            parts = (fetched[:, 0:128], fetched[:, 128:256], dot(hot, pool_tail[s]) * weight)
            for t in range(3):
                if f % 2 == 0:
                    moved = jnp.where(cell == 0, pltpu.roll(parts[t], 128 - 3 * stride, 1), 0.0)
                else:
                    moved = jnp.where(cell == 3, pltpu.roll(parts[t], 3 * stride, 1), 0.0)
                tiles[t] = tiles[t] + moved
        value[...] = value[...] - jnp.concatenate(tiles, axis=1)

        for copy in donor_copies:
            copy.wait_recv()
        for g in range(GRP - 1):
            even, odd = spread(donor_in[s, 64 * g : 64 * g + 64, :])
            donor_tail[s, DONORS * g : DONORS * g + 64, :] = even
            donor_tail[s, DONORS * g + 64 : DONORS * g + 128, :] = odd
        done = donor_copies + halo_copies
        donor = jnp.concatenate([dot(donor_hot[...], donor_pool[s]), dot(donor_hot[...], donor_tail[s])], axis=1)
        fringe = donor[0:ROWS] * column(24) + donor[ROWS:] * column(25)
        value[...] = (value[...] - fringe) * inv_diag[...]
        if s == 0:
            stage(1, 0, value[0:DONORS, :])
            donor_copies = send_donors(1)
            stage(1, 1, value[DONORS:, :])
            halo_copies = send_halo(1)
        for copy in done:
            copy.wait_send()
    out[...] = jnp.transpose(value[...])[0:VALS, :]
    for copy in z_copies[1:] + d_copies:
        copy.wait_send()


def body(ckpt, rhs, npos, opos, lmat, rmat, fblk, fw, dblk, dw):
    args = (ckpt.T, rhs.T, npos.reshape(1, ROWS), opos.reshape(1, ROWS), lmat, rmat, fblk, fw, dblk, dw)
    dma = pltpu.SemaphoreType.DMA
    out = pl.pallas_call(
        kernel,
        out_shape=pltpu.VMEM((VALS, ROWS), F32),
        in_specs=[pl.BlockSpec(memory_space=pl.ANY)] * 10,
        out_specs=pl.BlockSpec(memory_space=pltpu.VMEM),
        scratch_shapes=[pltpu.VMEM(a.shape, a.dtype) for a in args]
        + [pltpu.VMEM((SLOTS, PACKED), BF16)] * 4
        + [
            pltpu.VMEM((128, ROWS), F32),
            pltpu.VMEM((6 * ROWS, 3 * ROWS), BF16),
            pltpu.VMEM((2 * ROWS, 3 * DONORS), BF16),
            pltpu.VMEM((2, 3 * ROWS, MAIN), BF16),
            pltpu.VMEM((2, 3 * ROWS, 128), BF16),
            pltpu.VMEM((2, DONORS, 128), BF16),
            pltpu.VMEM((2, 2, DONORS, 128), BF16),
            pltpu.VMEM((2, 3 * DONORS, MAIN), BF16),
            pltpu.VMEM((2, 3 * DONORS, 128), BF16),
            pltpu.VMEM((2, 3 * 64, 128), BF16),
            pltpu.VMEM((PADDED, 2 * PADDED), BF16),
            pltpu.VMEM((2 * PADDED, PADDED), BF16),
        ]
        + [pltpu.VMEM((ROWS, PADDED), F32)] * 5
        + [dma((len(args),))]
        + [dma((NZ - 1,))] * 2
        + [dma((CHUNKS * (ND - 1),))] * 2
        + [dma((2, 10))] * 2,
        compiler_params=pltpu.CompilerParams(collective_id=0, has_side_effects=True),
    )(*args)
    return out.T


def solution(mesh):
    row, vec, many = P(("blk", "grp"), None), P(("blk", "grp")), P(None, ("blk", "grp"))
    return jax.shard_map(
        body,
        mesh=mesh,
        in_specs=(row, row, vec, vec, P(), P(), many, many, many, many),
        out_specs=row,
        check_vma=False,
    )
```

```python
import jax
import jax.numpy as jnp
from jax import lax
from jax.experimental import pallas as pl
from jax.experimental.pallas import tpu as pltpu
from jax.sharding import PartitionSpec as P

MESH = pl.DeviceIdType.MESH
ROWS = 256
VALS = 320
MAIN = 256
PADDED = 384
PACKED = 640
BLK = 128
GRP = 4
NZ = 16
ND = 8
CAP = 4
SLOTS = BLK * CAP
DONORS = 128
PER_CHUNK = 2
CHUNKS = NZ // PER_CHUNK
CHUNK = SLOTS // CHUNKS
PIECE = ND * CAP
PART = PER_CHUNK * CAP
F32 = jnp.float32
BF16 = jnp.bfloat16
ORDER = (0, 8, 9, 7, 10, 6, 11, 5, 12, 4, 13, 3, 15, 1, 14, 2)


def dot(a, b):
    return jnp.dot(a, b, preferred_element_type=F32)


def dot_t(a, b):
    return lax.dot_general(a, b, (((1,), (1,)), ((), ())), preferred_element_type=F32)


def iota(shape, dim):
    return lax.broadcasted_iota(jnp.int32, shape, dim)


def place_of(away):
    away = away & (NZ - 1)
    return sum(jnp.where(away == a, p, 0) for p, a in enumerate(ORDER) if p)


def arrived(ref, sem):
    pltpu.make_async_copy(ref, ref, sem).wait()


def remote(src, dst, send_sem, recv_sem, **where):
    return pltpu.make_async_remote_copy(
        src_ref=src, dst_ref=dst, send_sem=send_sem, recv_sem=recv_sem, device_id=where, device_id_type=MESH
    )


def kernel(
    ckpt_hbm, rhs_hbm, npos_hbm, opos_hbm, lmat_hbm, rmat_hbm, fblk_hbm, fw_hbm, dblk_hbm, dw_hbm, out,
    ckpt, rhs, npos, opos, lmat, rmat, fblk, fw, dblk, dw,
    send, zrecv, zpack, got, table,
    own_hot, own_tail_hot, halo_hot, halo_tail_hot, donor_hot, donor_tail_hot,
    own, own_tail, halo, halo_tail, donor_pool, donor_tail, mats_a, mats_b,
    left_gain, right_gain, inv_diag, rhs_f, value,
    in_sem, zs_sem, zr_sem, ds_sem, dr_sem, hs_sem, hr_sem,
):
    me = lax.axis_index("blk")
    grp = lax.axis_index("grp")
    my_z, my_d = me // ND, me % ND
    below, above = (me + BLK - 1) % BLK, (me + 1) % BLK

    barrier = pltpu.get_barrier_semaphore()

    def greet(**where):
        pl.semaphore_signal(barrier, inc=1, device_id=where, device_id_type=MESH)

    for away in (8, 7, 9, 6, 10, 5, 11, 4, 12, 3, 13, 2, 14, 1, 15):
        greet(blk=(my_z + away) % NZ * ND + my_d)
    for e in range(1, ND):
        greet(blk=my_z * ND + (my_d + e) % ND)
    for g in range(1, GRP):
        greet(grp=(grp + g) % GRP)
    greet(blk=below)
    greet(blk=above)

    pairs = (
        (npos_hbm, npos), (ckpt_hbm, ckpt), (rhs_hbm, rhs), (opos_hbm, opos), (fblk_hbm, fblk),
        (fw_hbm, fw), (dblk_hbm, dblk), (dw_hbm, dw), (lmat_hbm, lmat), (rmat_hbm, rmat),
    )
    loads = [pltpu.make_async_copy(a, b, in_sem.at[i]) for i, (a, b) in enumerate(pairs)]
    for load in loads:
        load.start()

    loads[0].wait()
    target = npos[...] >> 10
    key = place_of((target >> 3) - my_z) * ND + (((target & (ND - 1)) - my_d) & (ND - 1))
    hot = (key == iota((BLK, ROWS), 0)).astype(BF16)
    earlier = (iota((ROWS, ROWS), 0) < iota((ROWS, ROWS), 1)).astype(BF16)
    rank = jnp.sum(hot.astype(F32) * dot(hot, earlier), axis=0, keepdims=True)
    slot = (key * CAP).astype(F32) + rank
    put = (slot == iota((SLOTS, ROWS), 0).astype(F32)).astype(BF16)
    loads[1].wait()
    loads[2].wait()
    tail = jnp.concatenate([ckpt[MAIN:VALS, :], rhs[MAIN:VALS, :]], axis=0)
    send[:, 0:256] = dot_t(put, ckpt[0:MAIN, :]).astype(BF16)
    send[:, 256:512] = dot_t(put, rhs[0:MAIN, :]).astype(BF16)
    send[:, 512:640] = dot_t(put, tail).astype(BF16)

    pl.semaphore_wait(barrier, NZ - 1 + ND - 1 + GRP - 1 + 2)

    for p in range(1, NZ):
        rows = pl.ds(p * PIECE, PIECE)
        to = (my_z + ORDER[p]) % NZ * ND + my_d
        remote(send.at[rows], zrecv.at[rows], zs_sem, zr_sem.at[p // PER_CHUNK], blk=to).start()
    zrecv[0:PIECE, :] = send[0:PIECE, :]

    row, col = iota((CHUNK, CHUNK), 0), iota((CHUNK, CHUNK), 1)
    regroup = (col == ((row // CAP) % PER_CHUNK) * PIECE + (row // PART) * CAP + row % CAP).astype(BF16)

    def pass_on(q):
        rows = slice(q * CHUNK, (q + 1) * CHUNK)
        sent = PIECE if q == 0 else 0
        arrived(zrecv.at[pl.ds(q * CHUNK + sent, CHUNK - sent)], zr_sem.at[q])
        moved = dot(regroup, zrecv[rows, :]).astype(BF16)
        zpack[rows, :] = moved
        for e in (4, 5, 3, 2, 6, 7, 1):
            part = pl.ds(q * CHUNK + e * PART, PART)
            to = my_z * ND + (my_d + e) % ND
            remote(zpack.at[part], got.at[part], ds_sem, dr_sem, blk=to).start()
        got[q * CHUNK : q * CHUNK + PART, :] = moved[0:PART, :]

    for load in loads[3:]:
        load.wait()
    table[...] = jnp.zeros_like(table)
    faces = fblk[...]
    side = jnp.where(faces >= 0, ((faces >> 10) - me + 1) & (BLK - 1), -1)
    local = faces & (ROWS - 1)
    packed = ((local >> 7) << 6) + (local & 63)
    away_side = (side >> 1) & 1
    outer = (side == 0) | (side == 2)
    table[0:6, :] = jnp.where(outer, away_side * ROWS + local, -1).astype(F32)
    table[8:14, :] = fw[...]
    table[48:54, :] = jnp.where(side == 1, local, -1).astype(F32)
    table[56:62, :] = jnp.where(outer, away_side * DONORS + packed, -1).astype(F32)
    table[64:70, :] = jnp.where(side == 1, packed, -1).astype(F32)
    table[72:78, :] = ((local >> 6) & 1).astype(F32)
    donors = dblk[...]
    donor_grp = (((donors >> 8) - grp) & (GRP - 1)) - 1
    table[16:18, :] = (donor_grp * DONORS + (donors & (DONORS - 1))).astype(F32)
    table[80:82, :] = (donor_grp * 64 + (donors & 63)).astype(F32)
    table[88:90, :] = ((donors >> 6) & 1).astype(F32)
    table[24:26, :] = dw[...]
    anchor = opos[...] >> 10
    e = (my_d - (anchor & (ND - 1))) & (ND - 1)
    place = place_of(my_z - (anchor >> 3))
    order_row = ((place * ND + e) * ROWS + (opos[...] & (ROWS - 1))).astype(F32)
    base = (place // PER_CHUNK) * CHUNK + e * PART + (place % PER_CHUNK) * CAP
    table[32:33, :] = order_row
    table[40:41, :] = base.astype(F32)
    columns = jnp.transpose(table[...])

    def column(n):
        return columns[:, n : n + 1]

    smaller = (order_row < column(32)).astype(BF16)
    rank = dot(smaller, jnp.ones((ROWS, 128), BF16)).astype(jnp.int32) & (CAP - 1)
    recv_slot = rank.astype(F32) + column(40)
    lanes = iota((ROWS, 128), 1).astype(F32)
    pick = jnp.concatenate(
        [(recv_slot == lanes + 128.0 * t).astype(BF16) for t in range(SLOTS // 128)], axis=1
    )

    def select(ref, first, count):
        lane = iota((ROWS, ref.shape[1]), 1).astype(F32)
        for n in range(count):
            ref[n * ROWS : (n + 1) * ROWS, :] = (column(first + n) == lane).astype(BF16)

    select(halo_hot, 0, 6)
    select(own_hot, 48, 6)
    select(halo_tail_hot, 56, 6)
    select(own_tail_hot, 64, 6)
    select(donor_hot, 16, 2)
    select(donor_tail_hot, 80, 2)

    mats_a[...] = jnp.zeros_like(mats_a)
    mats_b[...] = jnp.zeros_like(mats_b)
    mats_a[0:VALS, 0:VALS] = lmat[...]
    mats_b[0:VALS, 0:VALS] = rmat[...]
    mats_a[:, PADDED:] = jnp.transpose(mats_b[0:PADDED, :])
    mats_b[PADDED:, :] = jnp.transpose(mats_a[:, 0:PADDED])

    for q in range(CHUNKS):
        pass_on(q)
    arrived(got.at[pl.ds(0, SLOTS - SLOTS // ND)], dr_sem)

    half = iota((ROWS, 128), 1) < 64
    last = dot(pick, got[:, 512:640])
    state = jnp.concatenate([dot(pick, got[:, 0:256]), jnp.where(half, last, 0.0)], axis=1)
    diag = 1.0 / (2.0 + state * state)
    inv_diag[...] = diag
    rhs_new = jnp.concatenate(
        [dot(pick, got[:, 256:512]), jnp.where(half, pltpu.roll(last, 64, 1), 0.0)], axis=1
    )
    rhs_f[...] = rhs_new
    value[...] = rhs_new * diag

    def stage(s, h, rows):
        own[s, DONORS * h : DONORS * (h + 1), :] = rows[:, 0:MAIN].astype(BF16)
        low, high = rows[0:64, MAIN:], rows[64:128, MAIN:]
        turned_low, turned_high = pltpu.roll(low, 64, 1), pltpu.roll(high, 64, 1)
        at = slice(64 * h, 64 * h + 64)
        own_tail[s, at, 0:128] = jnp.where(half[0:64], low, turned_high).astype(BF16)
        own_tail[s, at, 128:256] = jnp.where(half[0:64], high, turned_low).astype(BF16)

    def turn(ref, s):
        ref[s, :, 128:256] = pltpu.roll(ref[s, :, 0:128].astype(F32), 64, 1).astype(BF16)

    tail_lanes = pl.ds(0, 128)

    def send_donors(s):
        for g in (2, 1, 3):
            to = (grp + GRP - g) % GRP
            remote(
                own.at[s, pl.ds(0, DONORS)], donor_pool.at[s, pl.ds((g - 1) * DONORS, DONORS)],
                hs_sem.at[s, 2], hr_sem.at[s, 2], grp=to,
            ).start()
            remote(
                own_tail.at[s, pl.ds(0, 64), tail_lanes],
                donor_tail.at[s, pl.ds((g - 1) * 64, 64), tail_lanes],
                hs_sem.at[s, 3], hr_sem.at[s, 3], grp=to,
            ).start()

    def send_halo(s):
        for n, to in enumerate((above, below)):
            remote(
                own.at[s], halo.at[s, pl.ds(n * ROWS, ROWS)],
                hs_sem.at[s, 0], hr_sem.at[s, 0], blk=to,
            ).start()
            remote(
                own_tail.at[s, :, tail_lanes], halo_tail.at[s, pl.ds(n * DONORS, DONORS), tail_lanes],
                hs_sem.at[s, 1], hr_sem.at[s, 1], blk=to,
            ).start()

    def moves(s):
        return (halo.at[s], halo_tail.at[s, :, tail_lanes], donor_pool.at[s], donor_tail.at[s, :, tail_lanes])

    lane = iota((ROWS, 128), 1)

    def face_pass(main_hot, main, tail_hot, tail):
        tiles = [jnp.zeros((ROWS, 128), F32) for _ in range(3)]
        for f in range(6):
            stride = (16, 4, 1)[f // 2]
            cell = lane // stride % 4
            rows = slice(f * ROWS, (f + 1) * ROWS)
            weight = column(8 + f)
            fetched = dot(main_hot[rows, :], main)
            both = dot(tail_hot[rows, :], tail)
            last = jnp.where(column(72 + f) > 0.5, both[:, 128:256], both[:, 0:128])
            for t, part in enumerate((fetched[:, 0:128], fetched[:, 128:256], last)):
                if f % 2 == 0:
                    moved = jnp.where(cell == 0, pltpu.roll(part * weight, 128 - 3 * stride, 1), 0.0)
                else:
                    moved = jnp.where(cell == 3, pltpu.roll(part * weight, 3 * stride, 1), 0.0)
                tiles[t] = tiles[t] + moved
        return jnp.concatenate(tiles, axis=1)

    stage(0, 0, value[0:DONORS, :])
    send_donors(0)
    stage(0, 1, value[DONORS:, :])
    send_halo(0)
    left_gain[...] = 0.5 * jnp.tanh(state)
    right_gain[...] = 0.4 * jnp.tanh(1.5 * state - 0.5)

    for s in range(2):
        rounded = value[...].astype(BF16)
        proj = dot(rounded, mats_a[...])
        mid_l = (proj[:, 0:PADDED] * left_gain[...]).astype(BF16)
        mid_r = (proj[:, PADDED:] * right_gain[...]).astype(BF16)
        applied = dot(mid_l, mats_b[0:PADDED, :]) + dot(mid_r, mats_b[PADDED:, :])
        value[...] = rhs_f[...] - applied
        value[...] = value[...] - face_pass(own_hot, own[s], own_tail_hot, own_tail[s])

        for n in (0, 1):
            arrived(moves(s)[n], hr_sem.at[s, n])
        turn(halo_tail, s)
        value[...] = value[...] - face_pass(halo_hot, halo[s], halo_tail_hot, halo_tail[s])

        for n in (2, 3):
            arrived(moves(s)[n], hr_sem.at[s, n])
        turn(donor_tail, s)
        main = dot(donor_hot[...], donor_pool[s])
        both = dot(donor_tail_hot[...], donor_tail[s])
        fringe = jnp.zeros((ROWS, PADDED), F32)
        for k in range(2):
            rows = slice(k * ROWS, (k + 1) * ROWS)
            last = jnp.where(column(88 + k) > 0.5, both[rows, 128:256], both[rows, 0:128])
            fringe = fringe + jnp.concatenate([main[rows], last], axis=1) * column(24 + k)
        value[...] = (value[...] - fringe) * inv_diag[...]
        if s == 0:
            stage(1, 0, value[0:DONORS, :])
            send_donors(1)
            stage(1, 1, value[DONORS:, :])
            send_halo(1)
    out[...] = jnp.transpose(value[...])[0:VALS, :]
    arrived(send.at[pl.ds(PIECE, SLOTS - PIECE)], zs_sem)
    arrived(zpack.at[pl.ds(0, SLOTS - SLOTS // ND)], ds_sem)
    for s in range(2):
        for n, ref in enumerate(moves(s)):
            arrived(ref, hs_sem.at[s, n])


def body(ckpt, rhs, npos, opos, lmat, rmat, fblk, fw, dblk, dw):
    args = (ckpt.T, rhs.T, npos.reshape(1, ROWS), opos.reshape(1, ROWS), lmat, rmat, fblk, fw, dblk, dw)
    dma = pltpu.SemaphoreType.DMA
    out = pl.pallas_call(
        kernel,
        out_shape=pltpu.VMEM((VALS, ROWS), F32),
        in_specs=[pl.BlockSpec(memory_space=pl.ANY)] * 10,
        out_specs=pl.BlockSpec(memory_space=pltpu.VMEM),
        scratch_shapes=[pltpu.VMEM(a.shape, a.dtype) for a in args]
        + [pltpu.VMEM((SLOTS, PACKED), BF16)] * 4
        + [
            pltpu.VMEM((128, ROWS), F32),
            pltpu.VMEM((6 * ROWS, ROWS), BF16),
            pltpu.VMEM((6 * ROWS, DONORS), BF16),
            pltpu.VMEM((6 * ROWS, 2 * ROWS), BF16),
            pltpu.VMEM((6 * ROWS, 2 * DONORS), BF16),
            pltpu.VMEM((2 * ROWS, 3 * DONORS), BF16),
            pltpu.VMEM((2 * ROWS, 3 * 64), BF16),
            pltpu.VMEM((2, ROWS, MAIN), BF16),
            pltpu.VMEM((2, DONORS, 256), BF16),
            pltpu.VMEM((2, 2 * ROWS, MAIN), BF16),
            pltpu.VMEM((2, 2 * DONORS, 256), BF16),
            pltpu.VMEM((2, 3 * DONORS, MAIN), BF16),
            pltpu.VMEM((2, 3 * 64, 256), BF16),
            pltpu.VMEM((PADDED, 2 * PADDED), BF16),
            pltpu.VMEM((2 * PADDED, PADDED), BF16),
        ]
        + [pltpu.VMEM((ROWS, PADDED), F32)] * 5
        + [dma((len(args),))]
        + [dma(()), dma((CHUNKS,)), dma(()), dma(())]
        + [dma((2, 4))] * 2,
        compiler_params=pltpu.CompilerParams(collective_id=0, has_side_effects=True),
    )(*args)
    return out.T


def solution(mesh):
    row, vec, many = P(("blk", "grp"), None), P(("blk", "grp")), P(None, ("blk", "grp"))
    return jax.shard_map(
        body,
        mesh=mesh,
        in_specs=(row, row, vec, vec, P(), P(), many, many, many, many),
        out_specs=row,
        check_vma=False,
    )
```

```python
import jax
import jax.numpy as jnp
from jax import lax
from jax.experimental import pallas as pl
from jax.experimental.pallas import tpu as pltpu
from jax.sharding import PartitionSpec as P

MESH = pl.DeviceIdType.MESH
ROWS = 256
VALS = 320
MAIN = 256
PADDED = 384
BLK = 128
GRP = 4
NZ = 16
ND = 8
CAP = 4
SLOTS = BLK * CAP
DONORS = 128
PIECE = ND * CAP
PART = NZ * CAP
WIDTHS = (256, 256, 128)
F32 = jnp.float32
BF16 = jnp.bfloat16
ORDER = (0, 8, 9, 7, 10, 6, 11, 5, 12, 4, 13, 3, 15, 1, 14, 2)


def dot(a, b):
    return jnp.dot(a, b, preferred_element_type=F32)


def dot_t(a, b):
    return lax.dot_general(a, b, (((1,), (1,)), ((), ())), preferred_element_type=F32)


def iota(shape, dim):
    return lax.broadcasted_iota(jnp.int32, shape, dim)


def place_of(away):
    away = away & (NZ - 1)
    return sum(jnp.where(away == a, p, 0) for p, a in enumerate(ORDER) if p)


def arrived(ref, sem):
    pltpu.make_async_copy(ref, ref, sem).wait()


def remote(src, dst, send_sem, recv_sem, **where):
    return pltpu.make_async_remote_copy(
        src_ref=src, dst_ref=dst, send_sem=send_sem, recv_sem=recv_sem, device_id=where, device_id_type=MESH
    )


def kernel(
    ckpt_hbm, rhs_hbm, npos_hbm, opos_hbm, lmat_hbm, rmat_hbm, fblk_hbm, fw_hbm, dblk_hbm, dw_hbm, out,
    ckpt, rhs, npos, opos, lmat, rmat, fblk, fw, dblk, dw,
    send_0, send_1, send_2, zrecv_0, zrecv_1, zrecv_2, zpack_0, zpack_1, zpack_2, got_0, got_1, got_2, table,
    own_hot, own_tail_hot, halo_hot, halo_tail_hot, donor_hot, donor_tail_hot,
    own, own_tail, halo, halo_tail, donor_pool, donor_tail, mats_a, mats_b,
    left_gain, right_gain, inv_diag, rhs_f, value, rest,
    in_sem, zs_sem, zr_sem, ds_sem, dr_sem, hs_sem, hr_sem,
):
    me = lax.axis_index("blk")
    grp = lax.axis_index("grp")
    my_z, my_d = me // ND, me % ND
    below, above = (me + BLK - 1) % BLK, (me + 1) % BLK

    send, zrecv = (send_0, send_1, send_2), (zrecv_0, zrecv_1, zrecv_2)
    zpack, got = (zpack_0, zpack_1, zpack_2), (got_0, got_1, got_2)

    barrier = pltpu.get_barrier_semaphore()

    def greet(**where):
        pl.semaphore_signal(barrier, inc=1, device_id=where, device_id_type=MESH)

    for away in (8, 7, 9, 6, 10, 5, 11, 4, 12, 3, 13, 2, 14, 1, 15):
        greet(blk=(my_z + away) % NZ * ND + my_d)
    for e in range(1, ND):
        greet(blk=my_z * ND + (my_d + e) % ND)
    for g in range(1, GRP):
        greet(grp=(grp + g) % GRP)
    greet(blk=below)
    greet(blk=above)

    pairs = (
        (npos_hbm, npos), (ckpt_hbm, ckpt), (rhs_hbm, rhs), (opos_hbm, opos), (fblk_hbm, fblk),
        (fw_hbm, fw), (dblk_hbm, dblk), (dw_hbm, dw), (lmat_hbm, lmat), (rmat_hbm, rmat),
    )
    loads = [pltpu.make_async_copy(a, b, in_sem.at[i]) for i, (a, b) in enumerate(pairs)]
    for load in loads:
        load.start()

    loads[0].wait()
    target = npos[...] >> 10
    key = place_of((target >> 3) - my_z) * ND + (((target & (ND - 1)) - my_d) & (ND - 1))
    hot = (key == iota((BLK, ROWS), 0)).astype(BF16)
    earlier = (iota((ROWS, ROWS), 0) < iota((ROWS, ROWS), 1)).astype(BF16)
    rank = jnp.sum(hot.astype(F32) * dot(hot, earlier), axis=0, keepdims=True)
    slot = (key * CAP).astype(F32) + rank
    put = (slot == iota((SLOTS, ROWS), 0).astype(F32)).astype(BF16)
    loads[1].wait()
    loads[2].wait()

    def pack(c):
        last = c == 2
        count = VALS - MAIN if last else 128
        at = slice(128 * c, 128 * c + count)
        both = jnp.concatenate([ckpt[at, :], rhs[at, :]], axis=0)
        send[c][...] = dot_t(put, both).astype(BF16)

    def send_z(c):
        for p in range(1, NZ):
            rows = pl.ds(p * PIECE, PIECE)
            to = (my_z + ORDER[p]) % NZ * ND + my_d
            remote(send[c].at[rows], zrecv[c].at[rows], zs_sem.at[c], zr_sem.at[c], blk=to).start()
        zrecv[c][0:PIECE, :] = send[c][0:PIECE, :]

    pack(0)
    pl.semaphore_wait(barrier, NZ - 1 + ND - 1 + GRP - 1 + 2)
    send_z(0)
    for c in (1, 2):
        pack(c)
        send_z(c)

    row, col = iota((SLOTS, SLOTS), 0), iota((SLOTS, SLOTS), 1)
    regroup = (col == ((row // CAP) % NZ) * PIECE + (row // PART) * CAP + row % CAP).astype(BF16)
    sent_z, sent_d = pl.ds(PIECE, SLOTS - PIECE), pl.ds(PART, SLOTS - PART)

    def pass_on(c):
        arrived(zrecv[c].at[sent_z], zr_sem.at[c])
        moved = dot(regroup, zrecv[c][...]).astype(BF16)
        zpack[c][...] = moved
        for e in (4, 5, 3, 2, 6, 7, 1):
            part = pl.ds(e * PART, PART)
            to = my_z * ND + (my_d + e) % ND
            remote(zpack[c].at[part], got[c].at[part], ds_sem.at[c], dr_sem.at[c], blk=to).start()
        got[c][0:PART, :] = moved[0:PART, :]

    for load in loads[3:]:
        load.wait()
    table[...] = jnp.zeros_like(table)
    faces = fblk[...]
    side = jnp.where(faces >= 0, ((faces >> 10) - me + 1) & (BLK - 1), -1)
    local = faces & (ROWS - 1)
    packed = ((local >> 7) << 6) + (local & 63)
    away_side = (side >> 1) & 1
    outer = (side == 0) | (side == 2)
    table[0:6, :] = jnp.where(outer, away_side * ROWS + local, -1).astype(F32)
    table[8:14, :] = fw[...]
    table[48:54, :] = jnp.where(side == 1, local, -1).astype(F32)
    table[56:62, :] = jnp.where(outer, away_side * DONORS + packed, -1).astype(F32)
    table[64:70, :] = jnp.where(side == 1, packed, -1).astype(F32)
    table[72:78, :] = ((local >> 6) & 1).astype(F32)
    donors = dblk[...]
    donor_grp = (((donors >> 8) - grp) & (GRP - 1)) - 1
    table[16:18, :] = (donor_grp * DONORS + (donors & (DONORS - 1))).astype(F32)
    table[80:82, :] = (donor_grp * 64 + (donors & 63)).astype(F32)
    table[88:90, :] = ((donors >> 6) & 1).astype(F32)
    table[24:26, :] = dw[...]
    anchor = opos[...] >> 10
    e = (my_d - (anchor & (ND - 1))) & (ND - 1)
    place = place_of(my_z - (anchor >> 3))
    order_row = ((place * ND + e) * ROWS + (opos[...] & (ROWS - 1))).astype(F32)
    base = e * PART + place * CAP
    table[32:33, :] = order_row
    table[40:41, :] = base.astype(F32)
    columns = jnp.transpose(table[...])

    def column(n):
        return columns[:, n : n + 1]

    smaller = (order_row < column(32)).astype(BF16)
    rank = dot(smaller, jnp.ones((ROWS, 128), BF16)).astype(jnp.int32) & (CAP - 1)
    recv_slot = rank.astype(F32) + column(40)
    lanes = iota((ROWS, 128), 1).astype(F32)
    pick = jnp.concatenate(
        [(recv_slot == lanes + 128.0 * t).astype(BF16) for t in range(SLOTS // 128)], axis=1
    )

    def select(ref, first, count):
        lane = iota((ROWS, ref.shape[1]), 1).astype(F32)
        for n in range(count):
            ref[n * ROWS : (n + 1) * ROWS, :] = (column(first + n) == lane).astype(BF16)

    select(halo_hot, 0, 6)
    select(own_hot, 48, 6)
    select(halo_tail_hot, 56, 6)
    select(own_tail_hot, 64, 6)
    select(donor_hot, 16, 2)
    select(donor_tail_hot, 80, 2)

    mats_a[...] = jnp.zeros_like(mats_a)
    mats_b[...] = jnp.zeros_like(mats_b)
    mats_a[0:VALS, 0:VALS] = lmat[...]
    mats_b[0:VALS, 0:VALS] = rmat[...]
    mats_a[:, PADDED:] = jnp.transpose(mats_b[0:PADDED, :])
    mats_b[PADDED:, :] = jnp.transpose(mats_a[:, 0:PADDED])

    half = iota((ROWS, 128), 1) < 64

    def unpack(c):
        arrived(got[c].at[sent_d], dr_sem.at[c])
        both = dot(pick, got[c][...])
        if c == 2:
            state = jnp.where(half, both, 0.0)
            right_side = jnp.where(half, pltpu.roll(both, 64, 1), 0.0)
        else:
            state, right_side = both[:, 0:128], both[:, 128:256]
        at = slice(128 * c, 128 * c + 128)
        diag = 1.0 / (2.0 + state * state)
        inv_diag[:, at] = diag
        rhs_f[:, at] = right_side
        value[:, at] = right_side * diag
        return state

    def gains(c, state):
        at = slice(128 * c, 128 * c + 128)
        left_gain[:, at] = 0.5 * jnp.tanh(state)
        right_gain[:, at] = 0.4 * jnp.tanh(1.5 * state - 0.5)

    def stage_tail(s, h, tails):
        low, high = tails[0:64], tails[64:128]
        turned_low, turned_high = pltpu.roll(low, 64, 1), pltpu.roll(high, 64, 1)
        at = slice(64 * h, 64 * h + 64)
        own_tail[s, at, 0:128] = jnp.where(half[0:64], low, turned_high).astype(BF16)
        own_tail[s, at, 128:256] = jnp.where(half[0:64], high, turned_low).astype(BF16)

    def turn(ref, s):
        ref[s, :, 128:256] = pltpu.roll(ref[s, :, 0:128].astype(F32), 64, 1).astype(BF16)

    def lanes_of(t):
        return pl.ds(128 if t == 1 else 0, 128)

    def send_donors(s, t):
        src, dst, rows = (own_tail, donor_tail, 64) if t == 2 else (own, donor_pool, DONORS)
        for g in (2, 1, 3):
            remote(
                src.at[s, pl.ds(0, rows), lanes_of(t)],
                dst.at[s, pl.ds((g - 1) * rows, rows), lanes_of(t)],
                hs_sem.at[s, 3 + t], hr_sem.at[s, 3 + t], grp=(grp + GRP - g) % GRP,
            ).start()

    def send_halo(s, t):
        src, dst, rows = (own_tail, halo_tail, DONORS) if t == 2 else (own, halo, ROWS)
        for n, to in enumerate((above, below)):
            remote(
                src.at[s, :, lanes_of(t)], dst.at[s, pl.ds(n * rows, rows), lanes_of(t)],
                hs_sem.at[s, t], hr_sem.at[s, t], blk=to,
            ).start()

    def moved_bytes(s, n):
        ref = (halo, halo, halo_tail, donor_pool, donor_pool, donor_tail)[n]
        return ref.at[s, :, lanes_of(n % 3)]

    def received(s, n):
        arrived(moved_bytes(s, n), hr_sem.at[s, n])

    lane = iota((ROWS, 128), 1)

    def face_tile(f, part):
        stride = (16, 4, 1)[f // 2]
        cell = lane // stride % 4
        if f % 2 == 0:
            return jnp.where(cell == 0, pltpu.roll(part, 128 - 3 * stride, 1), 0.0)
        return jnp.where(cell == 3, pltpu.roll(part, 3 * stride, 1), 0.0)

    def faces_main(hot, rows_of):
        tiles = [jnp.zeros((ROWS, 128), F32) for _ in range(2)]
        for f in range(6):
            fetched = dot(hot[f * ROWS : (f + 1) * ROWS, :], rows_of) * column(8 + f)
            tiles = [tiles[t] + face_tile(f, fetched[:, 128 * t : 128 * t + 128]) for t in range(2)]
        return jnp.concatenate(tiles, axis=1)

    def faces_tail(hot, rows_of):
        total = jnp.zeros((ROWS, 128), F32)
        for f in range(6):
            both = dot(hot[f * ROWS : (f + 1) * ROWS, :], rows_of)
            picked = jnp.where(column(72 + f) > 0.5, both[:, 128:256], both[:, 0:128])
            total = total + face_tile(f, picked * column(8 + f))
        return total

    def fringe_main(s):
        fetched = dot(donor_hot[...], donor_pool[s])
        return fetched[0:ROWS] * column(24) + fetched[ROWS:] * column(25)

    def fringe_tail(s):
        turn(donor_tail, s)
        both = dot(donor_tail_hot[...], donor_tail[s])
        total = jnp.zeros((ROWS, 128), F32)
        for k in range(2):
            rows = slice(k * ROWS, (k + 1) * ROWS)
            picked = jnp.where(column(88 + k) > 0.5, both[rows, 128:256], both[rows, 0:128])
            total = total + picked * column(24 + k)
        return total

    def applied():
        proj = dot(value[...].astype(BF16), mats_a[...])
        mid_l = (proj[:, 0:PADDED] * left_gain[...]).astype(BF16)
        mid_r = (proj[:, PADDED:] * right_gain[...]).astype(BF16)
        return dot(mid_l, mats_b[0:PADDED, :]) + dot(mid_r, mats_b[PADDED:, :])

    for c in (0, 1):
        pass_on(c)
        state = unpack(c)
        own[0, :, 128 * c : 128 * c + 128] = value[:, 128 * c : 128 * c + 128].astype(BF16)
        send_donors(0, c)
        send_halo(0, c)
        gains(c, state)
    rest[:, 0:MAIN] = rhs_f[:, 0:MAIN] - faces_main(own_hot, own[0])
    pass_on(2)
    received(0, 0)
    received(0, 1)
    rest[:, 0:MAIN] = rest[:, 0:MAIN] - faces_main(halo_hot, halo[0])
    received(0, 3)
    received(0, 4)
    rest[:, 0:MAIN] = rest[:, 0:MAIN] - fringe_main(0)
    state = unpack(2)
    stage_tail(0, 0, value[0:DONORS, MAIN:])
    send_donors(0, 2)
    stage_tail(0, 1, value[DONORS:, MAIN:])
    send_halo(0, 2)
    gains(2, state)
    rest[:, MAIN:] = rhs_f[:, MAIN:] - faces_tail(own_tail_hot, own_tail[0])
    rest[...] = rest[...] - applied()
    received(0, 2)
    turn(halo_tail, 0)
    rest[:, MAIN:] = rest[:, MAIN:] - faces_tail(halo_tail_hot, halo_tail[0])
    received(0, 5)
    rest[:, MAIN:] = rest[:, MAIN:] - fringe_tail(0)
    value[...] = rest[...] * inv_diag[...]

    own[1] = value[:, 0:MAIN].astype(BF16)
    for h in range(2):
        stage_tail(1, h, value[DONORS * h : DONORS * (h + 1), MAIN:])
    for t in range(3):
        send_donors(1, t)
    for t in range(3):
        send_halo(1, t)
    rest[...] = rhs_f[...] - applied()
    rest[:, 0:MAIN] = rest[:, 0:MAIN] - faces_main(own_hot, own[1])
    rest[:, MAIN:] = rest[:, MAIN:] - faces_tail(own_tail_hot, own_tail[1])
    received(1, 0)
    received(1, 1)
    rest[:, 0:MAIN] = rest[:, 0:MAIN] - faces_main(halo_hot, halo[1])
    received(1, 2)
    turn(halo_tail, 1)
    rest[:, MAIN:] = rest[:, MAIN:] - faces_tail(halo_tail_hot, halo_tail[1])
    for n in (3, 4, 5):
        received(1, n)
    rest[:, 0:MAIN] = rest[:, 0:MAIN] - fringe_main(1)
    rest[:, MAIN:] = rest[:, MAIN:] - fringe_tail(1)
    value[...] = rest[...] * inv_diag[...]
    out[...] = jnp.transpose(value[...])[0:VALS, :]
    for c in range(3):
        arrived(send[c].at[sent_z], zs_sem.at[c])
        arrived(zpack[c].at[sent_d], ds_sem.at[c])
    for s in range(2):
        for n in range(6):
            arrived(moved_bytes(s, n), hs_sem.at[s, n])


def body(ckpt, rhs, npos, opos, lmat, rmat, fblk, fw, dblk, dw):
    args = (ckpt.T, rhs.T, npos.reshape(1, ROWS), opos.reshape(1, ROWS), lmat, rmat, fblk, fw, dblk, dw)
    dma = pltpu.SemaphoreType.DMA
    out = pl.pallas_call(
        kernel,
        out_shape=pltpu.VMEM((VALS, ROWS), F32),
        in_specs=[pl.BlockSpec(memory_space=pl.ANY)] * 10,
        out_specs=pl.BlockSpec(memory_space=pltpu.VMEM),
        scratch_shapes=[pltpu.VMEM(a.shape, a.dtype) for a in args]
        + [pltpu.VMEM((SLOTS, width), BF16) for _ in range(4) for width in WIDTHS]
        + [
            pltpu.VMEM((128, ROWS), F32),
            pltpu.VMEM((6 * ROWS, ROWS), BF16),
            pltpu.VMEM((6 * ROWS, DONORS), BF16),
            pltpu.VMEM((6 * ROWS, 2 * ROWS), BF16),
            pltpu.VMEM((6 * ROWS, 2 * DONORS), BF16),
            pltpu.VMEM((2 * ROWS, 3 * DONORS), BF16),
            pltpu.VMEM((2 * ROWS, 3 * 64), BF16),
            pltpu.VMEM((2, ROWS, MAIN), BF16),
            pltpu.VMEM((2, DONORS, 256), BF16),
            pltpu.VMEM((2, 2 * ROWS, MAIN), BF16),
            pltpu.VMEM((2, 2 * DONORS, 256), BF16),
            pltpu.VMEM((2, 3 * DONORS, MAIN), BF16),
            pltpu.VMEM((2, 3 * 64, 256), BF16),
            pltpu.VMEM((PADDED, 2 * PADDED), BF16),
            pltpu.VMEM((2 * PADDED, PADDED), BF16),
        ]
        + [pltpu.VMEM((ROWS, PADDED), F32)] * 6
        + [dma((len(args),))]
        + [dma((3,))] * 4
        + [dma((2, 6))] * 2,
        compiler_params=pltpu.CompilerParams(collective_id=0, has_side_effects=True),
    )(*args)
    return out.T


def solution(mesh):
    row, vec, many = P(("blk", "grp"), None), P(("blk", "grp")), P(None, ("blk", "grp"))
    return jax.shard_map(
        body,
        mesh=mesh,
        in_specs=(row, row, vec, vec, P(), P(), many, many, many, many),
        out_specs=row,
        check_vma=False,
    )
```

```python
import jax
import jax.numpy as jnp
from jax import lax
from jax.experimental import pallas as pl
from jax.experimental.pallas import tpu as pltpu
from jax.sharding import PartitionSpec as P

MESH = pl.DeviceIdType.MESH
ROWS = 256
VALS = 320
MAIN = 256
PADDED = 384
BLK = 128
GRP = 4
NZ = 16
ND = 8
CAP = 4
SLOTS = BLK * CAP
DONORS = 128
PIECE = ND * CAP
HALF = SLOTS // 2
PART = HALF // ND
WIDTHS = (256, 256, 128)
F32 = jnp.float32
BF16 = jnp.bfloat16
ORDER = (0, 8, 9, 7, 10, 6, 11, 5, 12, 4, 13, 3, 15, 1, 14, 2)


def dot(a, b):
    return jnp.dot(a, b, preferred_element_type=F32)


def dot_t(a, b):
    return lax.dot_general(a, b, (((1,), (1,)), ((), ())), preferred_element_type=F32)


def iota(shape, dim):
    return lax.broadcasted_iota(jnp.int32, shape, dim)


def place_of(away):
    away = away & (NZ - 1)
    return sum(jnp.where(away == a, p, 0) for p, a in enumerate(ORDER) if p)


def arrived(ref, sem):
    pltpu.make_async_copy(ref, ref, sem).wait()


def remote(src, dst, send_sem, recv_sem, **where):
    return pltpu.make_async_remote_copy(
        src_ref=src, dst_ref=dst, send_sem=send_sem, recv_sem=recv_sem, device_id=where, device_id_type=MESH
    )


def kernel(
    ckpt_hbm, rhs_hbm, npos_hbm, opos_hbm, lmat_hbm, rmat_hbm, fblk_hbm, fw_hbm, dblk_hbm, dw_hbm, out,
    ckpt, rhs, npos, opos, lmat, rmat, fblk, fw, dblk, dw,
    send_0, send_1, send_2, dgot_0, dgot_1, dgot_2, zpack_0, zpack_1, zpack_2, got_0, got_1, got_2, table,
    own_hot, own_tail_hot, halo_hot, halo_tail_hot, donor_hot, donor_tail_hot,
    own, own_tail, halo, halo_tail, donor_pool, donor_tail, mats_a, mats_b,
    left_gain, right_gain, inv_diag, rhs_f, value, rest,
    in_sem, zs_sem, zr_sem, ds_sem, dr_sem, hs_sem, hr_sem,
):
    me = lax.axis_index("blk")
    grp = lax.axis_index("grp")
    my_z, my_d = me // ND, me % ND
    below, above = (me + BLK - 1) % BLK, (me + 1) % BLK

    send, dgot = (send_0, send_1, send_2), (dgot_0, dgot_1, dgot_2)
    zpack, got = (zpack_0, zpack_1, zpack_2), (got_0, got_1, got_2)

    barrier = pltpu.get_barrier_semaphore()

    def greet(**where):
        pl.semaphore_signal(barrier, inc=1, device_id=where, device_id_type=MESH)

    for away in (8, 7, 9, 6, 10, 5, 11, 4, 12, 3, 13, 2, 14, 1, 15):
        greet(blk=(my_z + away) % NZ * ND + my_d)
    for e in range(1, ND):
        greet(blk=my_z * ND + (my_d + e) % ND)
    for g in range(1, GRP):
        greet(grp=(grp + g) % GRP)
    greet(blk=below)
    greet(blk=above)

    pairs = (
        (npos_hbm, npos), (ckpt_hbm, ckpt), (rhs_hbm, rhs), (opos_hbm, opos), (fblk_hbm, fblk),
        (fw_hbm, fw), (dblk_hbm, dblk), (dw_hbm, dw), (lmat_hbm, lmat), (rmat_hbm, rmat),
    )
    loads = [pltpu.make_async_copy(a, b, in_sem.at[i]) for i, (a, b) in enumerate(pairs)]
    for load in loads:
        load.start()

    loads[0].wait()
    target = npos[...] >> 10
    key = place_of((target >> 3) - my_z) * ND + (((target & (ND - 1)) - my_d) & (ND - 1))
    hot = (key == iota((BLK, ROWS), 0)).astype(BF16)
    earlier = (iota((ROWS, ROWS), 0) < iota((ROWS, ROWS), 1)).astype(BF16)
    rank = jnp.sum(hot.astype(F32) * dot(hot, earlier), axis=0, keepdims=True)
    at = (key >> 6) * HALF + (key & (ND - 1)) * PART + ((key >> 3) & 7) * CAP
    slot = at.astype(F32) + rank
    put = (slot == iota((SLOTS, ROWS), 0).astype(F32)).astype(BF16)
    loads[1].wait()
    loads[2].wait()

    def pack(c):
        last = c == 2
        count = VALS - MAIN if last else 128
        at = slice(128 * c, 128 * c + count)
        both = jnp.concatenate([ckpt[at, :], rhs[at, :]], axis=0)
        send[c][...] = dot_t(put, both).astype(BF16)

    def send_d(c):
        for h in range(2):
            for e in (4, 5, 3, 2, 6, 7, 1):
                part = pl.ds(h * HALF + e * PART, PART)
                to = my_z * ND + (my_d + e) % ND
                remote(send[c].at[part], dgot[c].at[part], ds_sem.at[c], dr_sem.at[c, h], blk=to).start()
            kept = slice(h * HALF, h * HALF + PART)
            dgot[c][kept, :] = send[c][kept, :]

    row, col = iota((HALF, HALF), 0), iota((HALF, HALF), 1)
    regroup = (col == ((row // CAP) % ND) * PART + (row // PIECE) * CAP + row % CAP).astype(BF16)
    sent_z, sent_d = pl.ds(PIECE, SLOTS - PIECE), pl.ds(2 * PART, SLOTS - 2 * PART)

    def send_z(c, h):
        arrived(dgot[c].at[pl.ds(0, HALF - PART)], dr_sem.at[c, h])
        rows = slice(h * HALF, (h + 1) * HALF)
        moved = dot(regroup, dgot[c][rows, :]).astype(BF16)
        zpack[c][rows, :] = moved
        for p in range(8 * h, 8 * h + 8):
            if p:
                part = pl.ds(p * PIECE, PIECE)
                to = (my_z + ORDER[p]) % NZ * ND + my_d
                remote(zpack[c].at[part], got[c].at[part], zs_sem.at[c], zr_sem.at[c], blk=to).start()
        if h == 0:
            got[c][0:PIECE, :] = moved[0:PIECE, :]

    pack(0)
    pl.semaphore_wait(barrier, NZ - 1 + ND - 1 + GRP - 1 + 2)
    send_d(0)
    for c in (1, 2):
        pack(c)
        send_d(c)
    send_z(0, 0)
    send_z(0, 1)

    for load in loads[3:]:
        load.wait()
    table[...] = jnp.zeros_like(table)
    faces = fblk[...]
    side = jnp.where(faces >= 0, ((faces >> 10) - me + 1) & (BLK - 1), -1)
    local = faces & (ROWS - 1)
    packed = ((local >> 7) << 6) + (local & 63)
    away_side = (side >> 1) & 1
    outer = (side == 0) | (side == 2)
    table[0:6, :] = jnp.where(outer, away_side * ROWS + local, -1).astype(F32)
    table[8:14, :] = fw[...]
    table[48:54, :] = jnp.where(side == 1, local, -1).astype(F32)
    table[56:62, :] = jnp.where(outer, away_side * DONORS + packed, -1).astype(F32)
    table[64:70, :] = jnp.where(side == 1, packed, -1).astype(F32)
    table[72:78, :] = ((local >> 6) & 1).astype(F32)
    donors = dblk[...]
    donor_grp = (((donors >> 8) - grp) & (GRP - 1)) - 1
    table[16:18, :] = (donor_grp * DONORS + (donors & (DONORS - 1))).astype(F32)
    table[80:82, :] = (donor_grp * 64 + (donors & 63)).astype(F32)
    table[88:90, :] = ((donors >> 6) & 1).astype(F32)
    table[24:26, :] = dw[...]
    anchor = opos[...] >> 10
    e = (my_d - (anchor & (ND - 1))) & (ND - 1)
    place = place_of(my_z - (anchor >> 3))
    order_row = ((place * ND + e) * ROWS + (opos[...] & (ROWS - 1))).astype(F32)
    base = place * PIECE + e * CAP
    table[32:33, :] = order_row
    table[40:41, :] = base.astype(F32)
    columns = jnp.transpose(table[...])

    def column(n):
        return columns[:, n : n + 1]

    smaller = (order_row < column(32)).astype(BF16)
    rank = dot(smaller, jnp.ones((ROWS, 128), BF16)).astype(jnp.int32) & (CAP - 1)
    recv_slot = rank.astype(F32) + column(40)
    lanes = iota((ROWS, 128), 1).astype(F32)
    pick = jnp.concatenate(
        [(recv_slot == lanes + 128.0 * t).astype(BF16) for t in range(SLOTS // 128)], axis=1
    )

    def select(ref, first, count):
        lane = iota((ROWS, ref.shape[1]), 1).astype(F32)
        for n in range(count):
            ref[n * ROWS : (n + 1) * ROWS, :] = (column(first + n) == lane).astype(BF16)

    select(halo_hot, 0, 6)
    select(own_hot, 48, 6)
    select(halo_tail_hot, 56, 6)
    select(own_tail_hot, 64, 6)
    select(donor_hot, 16, 2)
    select(donor_tail_hot, 80, 2)

    mats_a[...] = jnp.zeros_like(mats_a)
    mats_b[...] = jnp.zeros_like(mats_b)
    mats_a[0:VALS, 0:VALS] = lmat[...]
    mats_b[0:VALS, 0:VALS] = rmat[...]
    mats_a[:, PADDED:] = jnp.transpose(mats_b[0:PADDED, :])
    mats_b[PADDED:, :] = jnp.transpose(mats_a[:, 0:PADDED])

    half = iota((ROWS, 128), 1) < 64

    def unpack(c):
        arrived(got[c].at[sent_z], zr_sem.at[c])
        both = dot(pick, got[c][...])
        if c == 2:
            state = jnp.where(half, both, 0.0)
            right_side = jnp.where(half, pltpu.roll(both, 64, 1), 0.0)
        else:
            state, right_side = both[:, 0:128], both[:, 128:256]
        at = slice(128 * c, 128 * c + 128)
        diag = 1.0 / (2.0 + state * state)
        inv_diag[:, at] = diag
        rhs_f[:, at] = right_side
        value[:, at] = right_side * diag
        return state

    def gains(c, state):
        at = slice(128 * c, 128 * c + 128)
        left_gain[:, at] = 0.5 * jnp.tanh(state)
        right_gain[:, at] = 0.4 * jnp.tanh(1.5 * state - 0.5)

    def stage_tail(s, h, tails):
        low, high = tails[0:64], tails[64:128]
        turned_low, turned_high = pltpu.roll(low, 64, 1), pltpu.roll(high, 64, 1)
        at = slice(64 * h, 64 * h + 64)
        own_tail[s, at, 0:128] = jnp.where(half[0:64], low, turned_high).astype(BF16)
        own_tail[s, at, 128:256] = jnp.where(half[0:64], high, turned_low).astype(BF16)

    def turn(ref, s):
        ref[s, :, 128:256] = pltpu.roll(ref[s, :, 0:128].astype(F32), 64, 1).astype(BF16)

    def lanes_of(t):
        return pl.ds(128 if t == 1 else 0, 128)

    def send_donors(s, t):
        src, dst, rows = (own_tail, donor_tail, 64) if t == 2 else (own, donor_pool, DONORS)
        for g in (2, 1, 3):
            remote(
                src.at[s, pl.ds(0, rows), lanes_of(t)],
                dst.at[s, pl.ds((g - 1) * rows, rows), lanes_of(t)],
                hs_sem.at[s, 3 + t], hr_sem.at[s, 3 + t], grp=(grp + GRP - g) % GRP,
            ).start()

    def send_halo(s, t):
        src, dst, rows = (own_tail, halo_tail, DONORS) if t == 2 else (own, halo, ROWS)
        for n, to in enumerate((above, below)):
            remote(
                src.at[s, :, lanes_of(t)], dst.at[s, pl.ds(n * rows, rows), lanes_of(t)],
                hs_sem.at[s, t], hr_sem.at[s, t], blk=to,
            ).start()

    def moved_bytes(s, n):
        ref = (halo, halo, halo_tail, donor_pool, donor_pool, donor_tail)[n]
        return ref.at[s, :, lanes_of(n % 3)]

    def received(s, n):
        arrived(moved_bytes(s, n), hr_sem.at[s, n])

    lane = iota((ROWS, 128), 1)

    def face_tile(f, part):
        stride = (16, 4, 1)[f // 2]
        cell = lane // stride % 4
        if f % 2 == 0:
            return jnp.where(cell == 0, pltpu.roll(part, 128 - 3 * stride, 1), 0.0)
        return jnp.where(cell == 3, pltpu.roll(part, 3 * stride, 1), 0.0)

    def faces_main(hot, rows_of):
        tiles = [jnp.zeros((ROWS, 128), F32) for _ in range(2)]
        for f in range(6):
            fetched = dot(hot[f * ROWS : (f + 1) * ROWS, :], rows_of) * column(8 + f)
            tiles = [tiles[t] + face_tile(f, fetched[:, 128 * t : 128 * t + 128]) for t in range(2)]
        return jnp.concatenate(tiles, axis=1)

    def faces_tail(hot, rows_of):
        total = jnp.zeros((ROWS, 128), F32)
        for f in range(6):
            both = dot(hot[f * ROWS : (f + 1) * ROWS, :], rows_of)
            picked = jnp.where(column(72 + f) > 0.5, both[:, 128:256], both[:, 0:128])
            total = total + face_tile(f, picked * column(8 + f))
        return total

    def fringe_main(s):
        fetched = dot(donor_hot[...], donor_pool[s])
        return fetched[0:ROWS] * column(24) + fetched[ROWS:] * column(25)

    def fringe_tail(s):
        turn(donor_tail, s)
        both = dot(donor_tail_hot[...], donor_tail[s])
        total = jnp.zeros((ROWS, 128), F32)
        for k in range(2):
            rows = slice(k * ROWS, (k + 1) * ROWS)
            picked = jnp.where(column(88 + k) > 0.5, both[rows, 128:256], both[rows, 0:128])
            total = total + picked * column(24 + k)
        return total

    def applied():
        proj = dot(value[...].astype(BF16), mats_a[...])
        mid_l = (proj[:, 0:PADDED] * left_gain[...]).astype(BF16)
        mid_r = (proj[:, PADDED:] * right_gain[...]).astype(BF16)
        return dot(mid_l, mats_b[0:PADDED, :]) + dot(mid_r, mats_b[PADDED:, :])

    for c in (1, 2):
        send_z(c, 0)
        send_z(c, 1)

    for c in (0, 1):
        state = unpack(c)
        own[0, :, 128 * c : 128 * c + 128] = value[:, 128 * c : 128 * c + 128].astype(BF16)
        send_donors(0, c)
        send_halo(0, c)
        gains(c, state)
    rest[:, 0:MAIN] = rhs_f[:, 0:MAIN] - faces_main(own_hot, own[0])
    state = unpack(2)
    stage_tail(0, 0, value[0:DONORS, MAIN:])
    send_donors(0, 2)
    stage_tail(0, 1, value[DONORS:, MAIN:])
    send_halo(0, 2)
    gains(2, state)
    received(0, 0)
    received(0, 1)
    rest[:, 0:MAIN] = rest[:, 0:MAIN] - faces_main(halo_hot, halo[0])
    received(0, 3)
    received(0, 4)
    rest[:, 0:MAIN] = rest[:, 0:MAIN] - fringe_main(0)
    rest[:, MAIN:] = rhs_f[:, MAIN:] - faces_tail(own_tail_hot, own_tail[0])
    rest[...] = rest[...] - applied()
    received(0, 2)
    turn(halo_tail, 0)
    rest[:, MAIN:] = rest[:, MAIN:] - faces_tail(halo_tail_hot, halo_tail[0])
    received(0, 5)
    rest[:, MAIN:] = rest[:, MAIN:] - fringe_tail(0)
    value[...] = rest[...] * inv_diag[...]

    own[1] = value[:, 0:MAIN].astype(BF16)
    for h in range(2):
        stage_tail(1, h, value[DONORS * h : DONORS * (h + 1), MAIN:])
    for t in range(3):
        send_donors(1, t)
    for t in range(3):
        send_halo(1, t)
    rest[...] = rhs_f[...] - applied()
    rest[:, 0:MAIN] = rest[:, 0:MAIN] - faces_main(own_hot, own[1])
    rest[:, MAIN:] = rest[:, MAIN:] - faces_tail(own_tail_hot, own_tail[1])
    received(1, 0)
    received(1, 1)
    rest[:, 0:MAIN] = rest[:, 0:MAIN] - faces_main(halo_hot, halo[1])
    received(1, 2)
    turn(halo_tail, 1)
    rest[:, MAIN:] = rest[:, MAIN:] - faces_tail(halo_tail_hot, halo_tail[1])
    for n in (3, 4, 5):
        received(1, n)
    rest[:, 0:MAIN] = rest[:, 0:MAIN] - fringe_main(1)
    rest[:, MAIN:] = rest[:, MAIN:] - fringe_tail(1)
    value[...] = rest[...] * inv_diag[...]
    out[...] = jnp.transpose(value[...])[0:VALS, :]
    for c in range(3):
        arrived(send[c].at[sent_d], ds_sem.at[c])
        arrived(zpack[c].at[sent_z], zs_sem.at[c])
    for s in range(2):
        for n in range(6):
            arrived(moved_bytes(s, n), hs_sem.at[s, n])


def body(ckpt, rhs, npos, opos, lmat, rmat, fblk, fw, dblk, dw):
    args = (ckpt.T, rhs.T, npos.reshape(1, ROWS), opos.reshape(1, ROWS), lmat, rmat, fblk, fw, dblk, dw)
    dma = pltpu.SemaphoreType.DMA
    out = pl.pallas_call(
        kernel,
        out_shape=pltpu.VMEM((VALS, ROWS), F32),
        in_specs=[pl.BlockSpec(memory_space=pl.ANY)] * 10,
        out_specs=pl.BlockSpec(memory_space=pltpu.VMEM),
        scratch_shapes=[pltpu.VMEM(a.shape, a.dtype) for a in args]
        + [pltpu.VMEM((SLOTS, width), BF16) for _ in range(4) for width in WIDTHS]
        + [
            pltpu.VMEM((128, ROWS), F32),
            pltpu.VMEM((6 * ROWS, ROWS), BF16),
            pltpu.VMEM((6 * ROWS, DONORS), BF16),
            pltpu.VMEM((6 * ROWS, 2 * ROWS), BF16),
            pltpu.VMEM((6 * ROWS, 2 * DONORS), BF16),
            pltpu.VMEM((2 * ROWS, 3 * DONORS), BF16),
            pltpu.VMEM((2 * ROWS, 3 * 64), BF16),
            pltpu.VMEM((2, ROWS, MAIN), BF16),
            pltpu.VMEM((2, DONORS, 256), BF16),
            pltpu.VMEM((2, 2 * ROWS, MAIN), BF16),
            pltpu.VMEM((2, 2 * DONORS, 256), BF16),
            pltpu.VMEM((2, 3 * DONORS, MAIN), BF16),
            pltpu.VMEM((2, 3 * 64, 256), BF16),
            pltpu.VMEM((PADDED, 2 * PADDED), BF16),
            pltpu.VMEM((2 * PADDED, PADDED), BF16),
        ]
        + [pltpu.VMEM((ROWS, PADDED), F32)] * 6
        + [dma((len(args),))]
        + [dma((3,)), dma((3,)), dma((3,)), dma((3, 2))]
        + [dma((2, 6))] * 2,
        compiler_params=pltpu.CompilerParams(collective_id=0, has_side_effects=True),
    )(*args)
    return out.T


def solution(mesh):
    row, vec, many = P(("blk", "grp"), None), P(("blk", "grp")), P(None, ("blk", "grp"))
    return jax.shard_map(
        body,
        mesh=mesh,
        in_specs=(row, row, vec, vec, P(), P(), many, many, many, many),
        out_specs=row,
        check_vma=False,
    )
```

```python
import jax
import jax.numpy as jnp
from jax import lax
from jax.experimental import pallas as pl
from jax.experimental.pallas import tpu as pltpu
from jax.sharding import PartitionSpec as P

MESH = pl.DeviceIdType.MESH
ROWS = 256
VALS = 320
MAIN = 256
PADDED = 384
BLK = 128
GRP = 4
NZ = 16
ND = 8
CAP = 4
SLOTS = BLK * CAP
DONORS = 128
PIECE = ND * CAP
HALF = SLOTS // 2
PART = HALF // ND
WIDTHS = (256, 256, 128)
F32 = jnp.float32
BF16 = jnp.bfloat16
ORDER = (0, 8, 9, 7, 10, 6, 11, 5, 12, 4, 13, 3, 15, 1, 14, 2)


def dot(a, b):
    return jnp.dot(a, b, preferred_element_type=F32)


def dot_t(a, b):
    return lax.dot_general(a, b, (((1,), (1,)), ((), ())), preferred_element_type=F32)


def iota(shape, dim):
    return lax.broadcasted_iota(jnp.int32, shape, dim)


def place_of(away):
    away = away & (NZ - 1)
    return sum(jnp.where(away == a, p, 0) for p, a in enumerate(ORDER) if p)


def arrived(ref, sem):
    pltpu.make_async_copy(ref, ref, sem).wait()


def remote(src, dst, send_sem, recv_sem, **where):
    return pltpu.make_async_remote_copy(
        src_ref=src, dst_ref=dst, send_sem=send_sem, recv_sem=recv_sem, device_id=where, device_id_type=MESH
    )


def kernel(
    ckpt_hbm, rhs_hbm, npos_hbm, opos_hbm, lmat_hbm, rmat_hbm, fblk_hbm, fw_hbm, dblk_hbm, dw_hbm, out,
    ckpt, rhs, npos, opos, lmat, rmat, fblk, fw, dblk, dw,
    send_0, send_1, send_2, dgot_0, dgot_1, dgot_2, zpack_0, zpack_1, zpack_2, got_0, got_1, got_2, mid, mid_pack, table,
    own_hot, own_tail_hot, halo_hot, halo_tail_hot, donor_hot, donor_tail_hot,
    own, own_tail, halo, halo_tail, donor_pool, donor_tail, mats_a, mats_b,
    left_gain, right_gain, inv_diag, rhs_f, value, rest,
    in_sem, zs_sem, zr_sem, ds_sem, dr_sem, mid_sem, hs_sem, hr_sem,
):
    me = lax.axis_index("blk")
    grp = lax.axis_index("grp")
    my_z, my_d = me // ND, me % ND
    below, above = (me + BLK - 1) % BLK, (me + 1) % BLK

    send, dgot = (send_0, send_1, send_2), (dgot_0, dgot_1, dgot_2)
    zpack, got = (zpack_0, zpack_1, zpack_2), (got_0, got_1, got_2)

    barrier = pltpu.get_barrier_semaphore()

    def greet(**where):
        pl.semaphore_signal(barrier, inc=1, device_id=where, device_id_type=MESH)

    for away in (8, 7, 9, 6, 10, 5, 11, 4, 12, 3, 13, 2, 14, 1, 15):
        greet(blk=(my_z + away) % NZ * ND + my_d)
    for e in range(1, ND):
        greet(blk=my_z * ND + (my_d + e) % ND)
    for g in range(1, GRP):
        greet(grp=(grp + g) % GRP)
    greet(blk=below)
    greet(blk=above)

    pairs = (
        (npos_hbm, npos), (ckpt_hbm, ckpt), (rhs_hbm, rhs), (opos_hbm, opos), (fblk_hbm, fblk),
        (fw_hbm, fw), (dblk_hbm, dblk), (dw_hbm, dw), (lmat_hbm, lmat), (rmat_hbm, rmat),
    )
    loads = [pltpu.make_async_copy(a, b, in_sem.at[i]) for i, (a, b) in enumerate(pairs)]
    for load in loads:
        load.start()

    loads[0].wait()
    target = npos[...] >> 10
    key = place_of((target >> 3) - my_z) * ND + (((target & (ND - 1)) - my_d) & (ND - 1))
    hot = (key == iota((BLK, ROWS), 0)).astype(BF16)
    earlier = (iota((ROWS, ROWS), 0) < iota((ROWS, ROWS), 1)).astype(BF16)
    rank = jnp.sum(hot.astype(F32) * dot(hot, earlier), axis=0, keepdims=True)
    at = (key >> 6) * HALF + (key & (ND - 1)) * PART + ((key >> 3) & 7) * CAP
    slots = iota((SLOTS, ROWS), 0).astype(F32)
    put = (at.astype(F32) + rank == slots).astype(BF16)
    at = jnp.where(key < BLK // 2, key * CAP, at)
    put_first = (at.astype(F32) + rank == slots).astype(BF16)
    loads[1].wait()
    loads[2].wait()

    def pack(c):
        last = c == 2
        count = VALS - MAIN if last else 128
        at = slice(128 * c, 128 * c + count)
        both = jnp.concatenate([ckpt[at, :], rhs[at, :]], axis=0)
        send[c][...] = dot_t(put if c else put_first, both).astype(BF16)

    def send_d(c):
        for h in range(2) if c else (1,):
            for e in (4, 5, 3, 2, 6, 7, 1):
                part = pl.ds(h * HALF + e * PART, PART)
                to = my_z * ND + (my_d + e) % ND
                remote(send[c].at[part], dgot[c].at[part], ds_sem.at[c], dr_sem.at[c, h], blk=to).start()
            kept = slice(h * HALF, h * HALF + PART)
            dgot[c][kept, :] = send[c][kept, :]

    row, col = iota((HALF, HALF), 0), iota((HALF, HALF), 1)
    regroup = (col == ((row // CAP) % ND) * PART + (row // PIECE) * CAP + row % CAP).astype(BF16)
    sent_z, sent_d = pl.ds(PIECE, SLOTS - PIECE), pl.ds(2 * PART, SLOTS - 2 * PART)

    def send_z(c, h):
        arrived(dgot[c].at[pl.ds(0, HALF - PART)], dr_sem.at[c, h])
        rows = slice(h * HALF, (h + 1) * HALF)
        moved = dot(regroup, dgot[c][rows, :]).astype(BF16)
        zpack[c][rows, :] = moved
        for p in range(8 * h, 8 * h + 8):
            if p:
                part = pl.ds(p * PIECE, PIECE)
                to = (my_z + ORDER[p]) % NZ * ND + my_d
                remote(zpack[c].at[part], got[c].at[part], zs_sem.at[c], zr_sem.at[c], blk=to).start()
        if h == 0:
            got[c][0:PIECE, :] = moved[0:PIECE, :]

    half_rows, half_sent = pl.ds(HALF, HALF), pl.ds(PIECE, HALF - PIECE)

    def first_z():
        for p in range(1, 8):
            part = pl.ds(p * PIECE, PIECE)
            to = (my_z + ORDER[p]) % NZ * ND + my_d
            remote(send[0].at[part], mid.at[part], mid_sem.at[0], mid_sem.at[1], blk=to).start()
        mid[0:PIECE, :] = send[0][0:PIECE, :]

    def first_d():
        arrived(mid.at[half_sent], mid_sem.at[1])
        back = (col == ((row // CAP) % ND) * PIECE + (row // PART) * CAP + row % CAP).astype(BF16)
        moved = dot(back, mid[...]).astype(BF16)
        mid_pack[...] = moved
        for e in (4, 5, 3, 2, 6, 7, 1):
            part = pl.ds(e * PART, PART)
            to = my_z * ND + (my_d + e) % ND
            remote(mid_pack.at[part], got[0].at[part], mid_sem.at[2], mid_sem.at[3], blk=to).start()
        got[0][0:PART, :] = moved[0:PART, :]

    pack(0)
    pl.semaphore_wait(barrier, NZ - 1 + ND - 1 + GRP - 1 + 2)
    first_z()
    send_d(0)
    for c in (1, 2):
        pack(c)
        send_d(c)

    for load in loads[3:]:
        load.wait()
    table[...] = jnp.zeros_like(table)
    faces = fblk[...]
    side = jnp.where(faces >= 0, ((faces >> 10) - me + 1) & (BLK - 1), -1)
    local = faces & (ROWS - 1)
    packed = ((local >> 7) << 6) + (local & 63)
    away_side = (side >> 1) & 1
    outer = (side == 0) | (side == 2)
    table[0:6, :] = jnp.where(outer, away_side * ROWS + local, -1).astype(F32)
    table[8:14, :] = fw[...]
    table[48:54, :] = jnp.where(side == 1, local, -1).astype(F32)
    table[56:62, :] = jnp.where(outer, away_side * DONORS + packed, -1).astype(F32)
    table[64:70, :] = jnp.where(side == 1, packed, -1).astype(F32)
    table[72:78, :] = ((local >> 6) & 1).astype(F32)
    donors = dblk[...]
    donor_grp = (((donors >> 8) - grp) & (GRP - 1)) - 1
    table[16:18, :] = (donor_grp * DONORS + (donors & (DONORS - 1))).astype(F32)
    table[80:82, :] = (donor_grp * 64 + (donors & 63)).astype(F32)
    table[88:90, :] = ((donors >> 6) & 1).astype(F32)
    table[24:26, :] = dw[...]
    anchor = opos[...] >> 10
    e = (my_d - (anchor & (ND - 1))) & (ND - 1)
    place = place_of(my_z - (anchor >> 3))
    order_row = ((place * ND + e) * ROWS + (opos[...] & (ROWS - 1))).astype(F32)
    base = place * PIECE + e * CAP
    table[32:33, :] = order_row
    table[40:41, :] = base.astype(F32)
    table[41:42, :] = jnp.where(place < ND, e * PART + place * CAP, base).astype(F32)
    columns = jnp.transpose(table[...])

    def column(n):
        return columns[:, n : n + 1]

    smaller = (order_row < column(32)).astype(BF16)
    rank = dot(smaller, jnp.ones((ROWS, 128), BF16)).astype(jnp.int32) & (CAP - 1)
    lanes = iota((ROWS, 128), 1).astype(F32)

    def picks(n):
        recv_slot = rank.astype(F32) + column(n)
        return jnp.concatenate(
            [(recv_slot == lanes + 128.0 * t).astype(BF16) for t in range(SLOTS // 128)], axis=1
        )

    pick, pick_first = picks(40), picks(41)

    def select(ref, first, count):
        lane = iota((ROWS, ref.shape[1]), 1).astype(F32)
        for n in range(count):
            ref[n * ROWS : (n + 1) * ROWS, :] = (column(first + n) == lane).astype(BF16)

    select(halo_hot, 0, 6)
    select(own_hot, 48, 6)
    select(halo_tail_hot, 56, 6)
    select(own_tail_hot, 64, 6)
    select(donor_hot, 16, 2)
    select(donor_tail_hot, 80, 2)

    mats_a[...] = jnp.zeros_like(mats_a)
    mats_b[...] = jnp.zeros_like(mats_b)
    mats_a[0:VALS, 0:VALS] = lmat[...]
    mats_b[0:VALS, 0:VALS] = rmat[...]
    mats_a[:, PADDED:] = jnp.transpose(mats_b[0:PADDED, :])
    mats_b[PADDED:, :] = jnp.transpose(mats_a[:, 0:PADDED])

    half = iota((ROWS, 128), 1) < 64

    def unpack(c):
        arrived(got[c].at[sent_z if c else half_rows], zr_sem.at[c])
        if c == 0:
            arrived(got[0].at[pl.ds(PART, HALF - PART)], mid_sem.at[3])
        both = dot(pick if c else pick_first, got[c][...])
        if c == 2:
            state = jnp.where(half, both, 0.0)
            right_side = jnp.where(half, pltpu.roll(both, 64, 1), 0.0)
        else:
            state, right_side = both[:, 0:128], both[:, 128:256]
        at = slice(128 * c, 128 * c + 128)
        diag = 1.0 / (2.0 + state * state)
        inv_diag[:, at] = diag
        rhs_f[:, at] = right_side
        value[:, at] = right_side * diag
        return state

    def gains(c, state):
        at = slice(128 * c, 128 * c + 128)
        left_gain[:, at] = 0.5 * jnp.tanh(state)
        right_gain[:, at] = 0.4 * jnp.tanh(1.5 * state - 0.5)

    def stage_tail(s, h, tails):
        low, high = tails[0:64], tails[64:128]
        turned_low, turned_high = pltpu.roll(low, 64, 1), pltpu.roll(high, 64, 1)
        at = slice(64 * h, 64 * h + 64)
        own_tail[s, at, 0:128] = jnp.where(half[0:64], low, turned_high).astype(BF16)
        own_tail[s, at, 128:256] = jnp.where(half[0:64], high, turned_low).astype(BF16)

    def turn(ref, s):
        ref[s, :, 128:256] = pltpu.roll(ref[s, :, 0:128].astype(F32), 64, 1).astype(BF16)

    def lanes_of(t):
        return pl.ds(128 if t == 1 else 0, 128)

    def send_donors(s, t):
        src, dst, rows = (own_tail, donor_tail, 64) if t == 2 else (own, donor_pool, DONORS)
        for g in (2, 1, 3):
            remote(
                src.at[s, pl.ds(0, rows), lanes_of(t)],
                dst.at[s, pl.ds((g - 1) * rows, rows), lanes_of(t)],
                hs_sem.at[s, 3 + t], hr_sem.at[s, 3 + t], grp=(grp + GRP - g) % GRP,
            ).start()

    def send_halo(s, t):
        src, dst, rows = (own_tail, halo_tail, DONORS) if t == 2 else (own, halo, ROWS)
        for n, to in enumerate((above, below)):
            remote(
                src.at[s, :, lanes_of(t)], dst.at[s, pl.ds(n * rows, rows), lanes_of(t)],
                hs_sem.at[s, t], hr_sem.at[s, t], blk=to,
            ).start()

    def moved_bytes(s, n):
        ref = (halo, halo, halo_tail, donor_pool, donor_pool, donor_tail)[n]
        return ref.at[s, :, lanes_of(n % 3)]

    def received(s, n):
        arrived(moved_bytes(s, n), hr_sem.at[s, n])

    lane = iota((ROWS, 128), 1)

    def face_tile(f, part):
        stride = (16, 4, 1)[f // 2]
        cell = lane // stride % 4
        if f % 2 == 0:
            return jnp.where(cell == 0, pltpu.roll(part, 128 - 3 * stride, 1), 0.0)
        return jnp.where(cell == 3, pltpu.roll(part, 3 * stride, 1), 0.0)

    def faces_main(hot, rows_of):
        tiles = [jnp.zeros((ROWS, 128), F32) for _ in range(2)]
        for f in range(6):
            fetched = dot(hot[f * ROWS : (f + 1) * ROWS, :], rows_of) * column(8 + f)
            tiles = [tiles[t] + face_tile(f, fetched[:, 128 * t : 128 * t + 128]) for t in range(2)]
        return jnp.concatenate(tiles, axis=1)

    def faces_tail(hot, rows_of):
        total = jnp.zeros((ROWS, 128), F32)
        for f in range(6):
            both = dot(hot[f * ROWS : (f + 1) * ROWS, :], rows_of)
            picked = jnp.where(column(72 + f) > 0.5, both[:, 128:256], both[:, 0:128])
            total = total + face_tile(f, picked * column(8 + f))
        return total

    def fringe_main(s):
        fetched = dot(donor_hot[...], donor_pool[s])
        return fetched[0:ROWS] * column(24) + fetched[ROWS:] * column(25)

    def fringe_tail(s):
        turn(donor_tail, s)
        both = dot(donor_tail_hot[...], donor_tail[s])
        total = jnp.zeros((ROWS, 128), F32)
        for k in range(2):
            rows = slice(k * ROWS, (k + 1) * ROWS)
            picked = jnp.where(column(88 + k) > 0.5, both[rows, 128:256], both[rows, 0:128])
            total = total + picked * column(24 + k)
        return total

    def applied():
        proj = dot(value[...].astype(BF16), mats_a[...])
        mid_l = (proj[:, 0:PADDED] * left_gain[...]).astype(BF16)
        mid_r = (proj[:, PADDED:] * right_gain[...]).astype(BF16)
        return dot(mid_l, mats_b[0:PADDED, :]) + dot(mid_r, mats_b[PADDED:, :])

    send_z(0, 1)
    for c in (1, 2):
        send_z(c, 0)
        send_z(c, 1)
    first_d()

    for c in (0, 1):
        state = unpack(c)
        own[0, :, 128 * c : 128 * c + 128] = value[:, 128 * c : 128 * c + 128].astype(BF16)
        send_donors(0, c)
        send_halo(0, c)
        gains(c, state)
    rest[:, 0:MAIN] = rhs_f[:, 0:MAIN] - faces_main(own_hot, own[0])
    state = unpack(2)
    stage_tail(0, 0, value[0:DONORS, MAIN:])
    send_donors(0, 2)
    stage_tail(0, 1, value[DONORS:, MAIN:])
    send_halo(0, 2)
    gains(2, state)
    received(0, 0)
    received(0, 1)
    rest[:, 0:MAIN] = rest[:, 0:MAIN] - faces_main(halo_hot, halo[0])
    received(0, 3)
    received(0, 4)
    rest[:, 0:MAIN] = rest[:, 0:MAIN] - fringe_main(0)
    rest[:, MAIN:] = rhs_f[:, MAIN:] - faces_tail(own_tail_hot, own_tail[0])
    rest[...] = rest[...] - applied()
    received(0, 2)
    turn(halo_tail, 0)
    rest[:, MAIN:] = rest[:, MAIN:] - faces_tail(halo_tail_hot, halo_tail[0])
    received(0, 5)
    rest[:, MAIN:] = rest[:, MAIN:] - fringe_tail(0)
    value[...] = rest[...] * inv_diag[...]

    own[1] = value[:, 0:MAIN].astype(BF16)
    for h in range(2):
        stage_tail(1, h, value[DONORS * h : DONORS * (h + 1), MAIN:])
    for t in range(3):
        send_donors(1, t)
    for t in range(3):
        send_halo(1, t)
    rest[...] = rhs_f[...] - applied()
    rest[:, 0:MAIN] = rest[:, 0:MAIN] - faces_main(own_hot, own[1])
    rest[:, MAIN:] = rest[:, MAIN:] - faces_tail(own_tail_hot, own_tail[1])
    received(1, 0)
    received(1, 1)
    rest[:, 0:MAIN] = rest[:, 0:MAIN] - faces_main(halo_hot, halo[1])
    received(1, 2)
    turn(halo_tail, 1)
    rest[:, MAIN:] = rest[:, MAIN:] - faces_tail(halo_tail_hot, halo_tail[1])
    for n in (3, 4, 5):
        received(1, n)
    rest[:, 0:MAIN] = rest[:, 0:MAIN] - fringe_main(1)
    rest[:, MAIN:] = rest[:, MAIN:] - fringe_tail(1)
    value[...] = rest[...] * inv_diag[...]
    out[...] = jnp.transpose(value[...])[0:VALS, :]
    for c in range(3):
        arrived(send[c].at[sent_d if c else pl.ds(0, HALF - PART)], ds_sem.at[c])
        arrived(zpack[c].at[sent_z if c else half_rows], zs_sem.at[c])
    arrived(mid.at[half_sent], mid_sem.at[0])
    arrived(mid_pack.at[pl.ds(PART, HALF - PART)], mid_sem.at[2])
    for s in range(2):
        for n in range(6):
            arrived(moved_bytes(s, n), hs_sem.at[s, n])


def body(ckpt, rhs, npos, opos, lmat, rmat, fblk, fw, dblk, dw):
    args = (ckpt.T, rhs.T, npos.reshape(1, ROWS), opos.reshape(1, ROWS), lmat, rmat, fblk, fw, dblk, dw)
    dma = pltpu.SemaphoreType.DMA
    out = pl.pallas_call(
        kernel,
        out_shape=pltpu.VMEM((VALS, ROWS), F32),
        in_specs=[pl.BlockSpec(memory_space=pl.ANY)] * 10,
        out_specs=pl.BlockSpec(memory_space=pltpu.VMEM),
        scratch_shapes=[pltpu.VMEM(a.shape, a.dtype) for a in args]
        + [pltpu.VMEM((SLOTS, width), BF16) for _ in range(4) for width in WIDTHS]
        + [pltpu.VMEM((HALF, WIDTHS[0]), BF16)] * 2
        + [
            pltpu.VMEM((128, ROWS), F32),
            pltpu.VMEM((6 * ROWS, ROWS), BF16),
            pltpu.VMEM((6 * ROWS, DONORS), BF16),
            pltpu.VMEM((6 * ROWS, 2 * ROWS), BF16),
            pltpu.VMEM((6 * ROWS, 2 * DONORS), BF16),
            pltpu.VMEM((2 * ROWS, 3 * DONORS), BF16),
            pltpu.VMEM((2 * ROWS, 3 * 64), BF16),
            pltpu.VMEM((2, ROWS, MAIN), BF16),
            pltpu.VMEM((2, DONORS, 256), BF16),
            pltpu.VMEM((2, 2 * ROWS, MAIN), BF16),
            pltpu.VMEM((2, 2 * DONORS, 256), BF16),
            pltpu.VMEM((2, 3 * DONORS, MAIN), BF16),
            pltpu.VMEM((2, 3 * 64, 256), BF16),
            pltpu.VMEM((PADDED, 2 * PADDED), BF16),
            pltpu.VMEM((2 * PADDED, PADDED), BF16),
        ]
        + [pltpu.VMEM((ROWS, PADDED), F32)] * 6
        + [dma((len(args),))]
        + [dma((3,)), dma((3,)), dma((3,)), dma((3, 2)), dma((4,))]
        + [dma((2, 6))] * 2,
        compiler_params=pltpu.CompilerParams(collective_id=0, has_side_effects=True),
    )(*args)
    return out.T


def solution(mesh):
    row, vec, many = P(("blk", "grp"), None), P(("blk", "grp")), P(None, ("blk", "grp"))
    return jax.shard_map(
        body,
        mesh=mesh,
        in_specs=(row, row, vec, vec, P(), P(), many, many, many, many),
        out_specs=row,
        check_vma=False,
    )
```

```python
import jax
import jax.numpy as jnp
from jax import lax
from jax.experimental import pallas as pl
from jax.experimental.pallas import tpu as pltpu
from jax.sharding import PartitionSpec as P

MESH = pl.DeviceIdType.MESH
ROWS = 256
VALS = 320
MAIN = 256
PADDED = 384
BLK = 128
GRP = 4
NZ = 16
ND = 8
CAP = 4
SLOTS = BLK * CAP
DONORS = 128
PIECE = ND * CAP
HALF = SLOTS // 2
PART = HALF // ND
WIDTHS = (256, 256, 128)
F32 = jnp.float32
BF16 = jnp.bfloat16
ORDER = (0, 8, 9, 7, 10, 6, 11, 5, 12, 4, 13, 3, 15, 1, 14, 2)


def dot(a, b):
    return jnp.dot(a, b, preferred_element_type=F32)


def dot_t(a, b):
    return lax.dot_general(a, b, (((1,), (1,)), ((), ())), preferred_element_type=F32)


def iota(shape, dim):
    return lax.broadcasted_iota(jnp.int32, shape, dim)


def place_of(away):
    away = away & (NZ - 1)
    return sum(jnp.where(away == a, p, 0) for p, a in enumerate(ORDER) if p)


def arrived(ref, sem):
    pltpu.make_async_copy(ref, ref, sem).wait()


def remote(src, dst, send_sem, recv_sem, **where):
    return pltpu.make_async_remote_copy(
        src_ref=src, dst_ref=dst, send_sem=send_sem, recv_sem=recv_sem, device_id=where, device_id_type=MESH
    )


def kernel(
    ckpt_hbm, rhs_hbm, npos_hbm, opos_hbm, lmat_hbm, rmat_hbm, fblk_hbm, fw_hbm, dblk_hbm, dw_hbm, out,
    ckpt, rhs, npos, opos, lmat, rmat, fblk, fw, dblk, dw,
    send_0, send_1, send_2, dgot_0, dgot_1, dgot_2, zpack_0, zpack_1, zpack_2, got_0, got_1, got_2, mid, mid_pack, table,
    own_hot, own_tail_hot, halo_hot, halo_tail_hot, donor_hot, donor_tail_hot,
    own, own_tail, halo, halo_tail, donor_pool, donor_tail, mats_a, mats_b,
    face_scale, low_scale, high_scale, donor_scale, donor_low, donor_high,
    left_gain, right_gain, inv_diag, rhs_f, value, rest,
    in_sem, zs_sem, zr_sem, ds_sem, dr_sem, mid_sem, hs_sem, hr_sem,
):
    me = lax.axis_index("blk")
    grp = lax.axis_index("grp")
    my_z, my_d = me // ND, me % ND
    below, above = (me + BLK - 1) % BLK, (me + 1) % BLK

    send, dgot = (send_0, send_1, send_2), (dgot_0, dgot_1, dgot_2)
    zpack, got = (zpack_0, zpack_1, zpack_2), (got_0, got_1, got_2)

    barrier = pltpu.get_barrier_semaphore()

    def greet(**where):
        pl.semaphore_signal(barrier, inc=1, device_id=where, device_id_type=MESH)

    for away in (8, 7, 9, 6, 10, 5, 11, 4, 12, 3, 13, 2, 14, 1, 15):
        greet(blk=(my_z + away) % NZ * ND + my_d)
    for e in range(1, ND):
        greet(blk=my_z * ND + (my_d + e) % ND)
    for g in range(1, GRP):
        greet(grp=(grp + g) % GRP)
    greet(blk=below)
    greet(blk=above)

    pairs = (
        (npos_hbm, npos), (ckpt_hbm, ckpt), (rhs_hbm, rhs), (opos_hbm, opos), (fblk_hbm, fblk),
        (fw_hbm, fw), (dblk_hbm, dblk), (dw_hbm, dw), (lmat_hbm, lmat), (rmat_hbm, rmat),
    )
    loads = [pltpu.make_async_copy(a, b, in_sem.at[i]) for i, (a, b) in enumerate(pairs)]
    for load in loads:
        load.start()

    loads[0].wait()
    target = npos[...] >> 10
    key = place_of((target >> 3) - my_z) * ND + (((target & (ND - 1)) - my_d) & (ND - 1))
    hot = (key == iota((BLK, ROWS), 0)).astype(BF16)
    earlier = (iota((ROWS, ROWS), 0) < iota((ROWS, ROWS), 1)).astype(BF16)
    rank = jnp.sum(hot.astype(F32) * dot(hot, earlier), axis=0, keepdims=True)
    at = (key >> 6) * HALF + (key & (ND - 1)) * PART + ((key >> 3) & 7) * CAP
    slots = iota((SLOTS, ROWS), 0).astype(F32)
    put = (at.astype(F32) + rank == slots).astype(BF16)
    at = jnp.where(key < BLK // 2, key * CAP, at)
    put_first = (at.astype(F32) + rank == slots).astype(BF16)
    loads[1].wait()
    loads[2].wait()

    def pack(c):
        last = c == 2
        count = VALS - MAIN if last else 128
        at = slice(128 * c, 128 * c + count)
        both = jnp.concatenate([ckpt[at, :], rhs[at, :]], axis=0)
        send[c][...] = dot_t(put if c else put_first, both).astype(BF16)

    def send_d(c):
        for h in range(2) if c else (1,):
            for e in (4, 5, 3, 2, 6, 7, 1):
                part = pl.ds(h * HALF + e * PART, PART)
                to = my_z * ND + (my_d + e) % ND
                remote(send[c].at[part], dgot[c].at[part], ds_sem.at[c], dr_sem.at[c, h], blk=to).start()
            kept = slice(h * HALF, h * HALF + PART)
            dgot[c][kept, :] = send[c][kept, :]

    row, col = iota((HALF, HALF), 0), iota((HALF, HALF), 1)
    regroup = (col == ((row // CAP) % ND) * PART + (row // PIECE) * CAP + row % CAP).astype(BF16)
    sent_z, sent_d = pl.ds(PIECE, SLOTS - PIECE), pl.ds(2 * PART, SLOTS - 2 * PART)

    def send_z(c, h):
        arrived(dgot[c].at[pl.ds(0, HALF - PART)], dr_sem.at[c, h])
        rows = slice(h * HALF, (h + 1) * HALF)
        moved = dot(regroup, dgot[c][rows, :]).astype(BF16)
        zpack[c][rows, :] = moved
        for p in range(8 * h, 8 * h + 8):
            if p:
                part = pl.ds(p * PIECE, PIECE)
                to = (my_z + ORDER[p]) % NZ * ND + my_d
                remote(zpack[c].at[part], got[c].at[part], zs_sem.at[c], zr_sem.at[c], blk=to).start()
        if h == 0:
            got[c][0:PIECE, :] = moved[0:PIECE, :]

    half_rows, half_sent = pl.ds(HALF, HALF), pl.ds(PIECE, HALF - PIECE)

    def first_z():
        for p in range(1, 8):
            part = pl.ds(p * PIECE, PIECE)
            to = (my_z + ORDER[p]) % NZ * ND + my_d
            remote(send[0].at[part], mid.at[part], mid_sem.at[0], mid_sem.at[1], blk=to).start()
        mid[0:PIECE, :] = send[0][0:PIECE, :]

    def first_d():
        arrived(mid.at[half_sent], mid_sem.at[1])
        back = (col == ((row // CAP) % ND) * PIECE + (row // PART) * CAP + row % CAP).astype(BF16)
        moved = dot(back, mid[...]).astype(BF16)
        mid_pack[...] = moved
        for e in (4, 5, 3, 2, 6, 7, 1):
            part = pl.ds(e * PART, PART)
            to = my_z * ND + (my_d + e) % ND
            remote(mid_pack.at[part], got[0].at[part], mid_sem.at[2], mid_sem.at[3], blk=to).start()
        got[0][0:PART, :] = moved[0:PART, :]

    pack(0)
    pl.semaphore_wait(barrier, NZ - 1 + ND - 1 + GRP - 1 + 2)
    first_z()
    send_d(0)
    for c in (1, 2):
        pack(c)
        send_d(c)

    for load in loads[3:]:
        load.wait()
    table[...] = jnp.zeros_like(table)
    faces = fblk[...]
    side = jnp.where(faces >= 0, ((faces >> 10) - me + 1) & (BLK - 1), -1)
    local = faces & (ROWS - 1)
    packed = ((local >> 7) << 6) + (local & 63)
    away_side = (side >> 1) & 1
    outer = (side == 0) | (side == 2)
    table[0:6, :] = jnp.where(outer, away_side * ROWS + local, -1).astype(F32)
    table[8:14, :] = fw[...]
    table[48:54, :] = jnp.where(side == 1, local, -1).astype(F32)
    table[56:62, :] = jnp.where(outer, away_side * DONORS + packed, -1).astype(F32)
    table[64:70, :] = jnp.where(side == 1, packed, -1).astype(F32)
    table[72:78, :] = ((local >> 6) & 1).astype(F32)
    donors = dblk[...]
    donor_grp = (((donors >> 8) - grp) & (GRP - 1)) - 1
    table[16:18, :] = (donor_grp * DONORS + (donors & (DONORS - 1))).astype(F32)
    table[80:82, :] = (donor_grp * 64 + (donors & 63)).astype(F32)
    table[88:90, :] = ((donors >> 6) & 1).astype(F32)
    table[24:26, :] = dw[...]
    anchor = opos[...] >> 10
    e = (my_d - (anchor & (ND - 1))) & (ND - 1)
    place = place_of(my_z - (anchor >> 3))
    order_row = ((place * ND + e) * ROWS + (opos[...] & (ROWS - 1))).astype(F32)
    base = place * PIECE + e * CAP
    table[32:33, :] = order_row
    table[40:41, :] = base.astype(F32)
    table[41:42, :] = jnp.where(place < ND, e * PART + place * CAP, base).astype(F32)
    columns = jnp.transpose(table[...])

    def column(n):
        return columns[:, n : n + 1]

    smaller = (order_row < column(32)).astype(BF16)
    rank = dot(smaller, jnp.ones((ROWS, 128), BF16)).astype(jnp.int32) & (CAP - 1)
    lanes = iota((ROWS, 128), 1).astype(F32)

    def picks(n):
        recv_slot = rank.astype(F32) + column(n)
        return jnp.concatenate(
            [(recv_slot == lanes + 128.0 * t).astype(BF16) for t in range(SLOTS // 128)], axis=1
        )

    pick, pick_first = picks(40), picks(41)

    def select(ref, first, count):
        lane = iota((ROWS, ref.shape[1]), 1).astype(F32)
        for n in range(count):
            ref[n * ROWS : (n + 1) * ROWS, :] = (column(first + n) == lane).astype(BF16)

    select(halo_hot, 0, 6)
    select(own_hot, 48, 6)
    select(halo_tail_hot, 56, 6)
    select(own_tail_hot, 64, 6)
    select(donor_hot, 16, 2)
    select(donor_tail_hot, 80, 2)

    lane = iota((ROWS, 128), 1)
    for f in range(6):
        cell = lane // (16, 4, 1)[f // 2] % 4
        scale = jnp.where(cell == (3 if f % 2 == 0 else 0), column(8 + f), 0.0)
        face_scale[f] = scale
        high = jnp.broadcast_to(column(72 + f), (ROWS, 128))
        low_scale[f] = jnp.where(high > 0.5, 0.0, scale)
        high_scale[f] = jnp.where(high > 0.5, scale, 0.0)
    for k in range(2):
        scale = jnp.broadcast_to(column(24 + k), (ROWS, 128))
        donor_scale[k] = scale
        high = jnp.broadcast_to(column(88 + k), (ROWS, 128))
        donor_low[k] = jnp.where(high > 0.5, 0.0, scale)
        donor_high[k] = jnp.where(high > 0.5, scale, 0.0)

    mats_a[...] = jnp.zeros_like(mats_a)
    mats_b[...] = jnp.zeros_like(mats_b)
    mats_a[0:VALS, 0:VALS] = lmat[...]
    mats_b[0:VALS, 0:VALS] = rmat[...]
    mats_a[:, PADDED:] = jnp.transpose(mats_b[0:PADDED, :])
    mats_b[PADDED:, :] = jnp.transpose(mats_a[:, 0:PADDED])

    half = iota((ROWS, 128), 1) < 64

    def unpack(c):
        arrived(got[c].at[sent_z if c else half_rows], zr_sem.at[c])
        if c == 0:
            arrived(got[0].at[pl.ds(PART, HALF - PART)], mid_sem.at[3])
        both = dot(pick if c else pick_first, got[c][...])
        if c == 2:
            state = jnp.where(half, both, 0.0)
            right_side = jnp.where(half, pltpu.roll(both, 64, 1), 0.0)
        else:
            state, right_side = both[:, 0:128], both[:, 128:256]
        at = slice(128 * c, 128 * c + 128)
        diag = 1.0 / (2.0 + state * state)
        inv_diag[:, at] = diag
        rhs_f[:, at] = right_side
        value[:, at] = right_side * diag
        return state

    def gains(c, state):
        at = slice(128 * c, 128 * c + 128)
        left_gain[:, at] = 0.5 * jnp.tanh(state)
        right_gain[:, at] = 0.4 * jnp.tanh(1.5 * state - 0.5)

    def stage_tail(s, h, tails):
        low, high = tails[0:64], tails[64:128]
        turned_low, turned_high = pltpu.roll(low, 64, 1), pltpu.roll(high, 64, 1)
        at = slice(64 * h, 64 * h + 64)
        own_tail[s, at, 0:128] = jnp.where(half[0:64], low, turned_high).astype(BF16)
        own_tail[s, at, 128:256] = jnp.where(half[0:64], high, turned_low).astype(BF16)

    def turn(ref, s):
        ref[s, :, 128:256] = pltpu.roll(ref[s, :, 0:128].astype(F32), 64, 1).astype(BF16)

    def lanes_of(t):
        return pl.ds(128 if t == 1 else 0, 128)

    def send_donors(s, t):
        src, dst, rows = (own_tail, donor_tail, 64) if t == 2 else (own, donor_pool, DONORS)
        for g in (2, 1, 3):
            remote(
                src.at[s, pl.ds(0, rows), lanes_of(t)],
                dst.at[s, pl.ds((g - 1) * rows, rows), lanes_of(t)],
                hs_sem.at[s, 3 + t], hr_sem.at[s, 3 + t], grp=(grp + GRP - g) % GRP,
            ).start()

    def send_halo(s, t):
        src, dst, rows = (own_tail, halo_tail, DONORS) if t == 2 else (own, halo, ROWS)
        for n, to in enumerate((above, below)):
            remote(
                src.at[s, :, lanes_of(t)], dst.at[s, pl.ds(n * rows, rows), lanes_of(t)],
                hs_sem.at[s, t], hr_sem.at[s, t], blk=to,
            ).start()

    def moved_bytes(s, n):
        ref = (halo, halo, halo_tail, donor_pool, donor_pool, donor_tail)[n]
        return ref.at[s, :, lanes_of(n % 3)]

    def received(s, n):
        arrived(moved_bytes(s, n), hr_sem.at[s, n])

    def placed(f, part):
        stride = (16, 4, 1)[f // 2]
        return pltpu.roll(part, 128 - 3 * stride if f % 2 == 0 else 3 * stride, 1)

    def faces_main(hot, rows_of):
        tiles = [jnp.zeros((ROWS, 128), F32) for _ in range(2)]
        for f in range(6):
            fetched = dot(hot[f * ROWS : (f + 1) * ROWS, :], rows_of)
            scale = face_scale[f]
            tiles = [tiles[t] + placed(f, fetched[:, 128 * t : 128 * t + 128] * scale) for t in range(2)]
        return jnp.concatenate(tiles, axis=1)

    def faces_tail(hot, rows_of):
        total = jnp.zeros((ROWS, 128), F32)
        for f in range(6):
            both = dot(hot[f * ROWS : (f + 1) * ROWS, :], rows_of)
            total = total + placed(f, both[:, 0:128] * low_scale[f] + both[:, 128:256] * high_scale[f])
        return total

    def fringe_main(s):
        total = [jnp.zeros((ROWS, 128), F32) for _ in range(2)]
        for k in range(2):
            fetched = dot(donor_hot[k * ROWS : (k + 1) * ROWS, :], donor_pool[s])
            scale = donor_scale[k]
            total = [total[t] + fetched[:, 128 * t : 128 * t + 128] * scale for t in range(2)]
        return jnp.concatenate(total, axis=1)

    def fringe_tail(s):
        turn(donor_tail, s)
        total = jnp.zeros((ROWS, 128), F32)
        for k in range(2):
            both = dot(donor_tail_hot[k * ROWS : (k + 1) * ROWS, :], donor_tail[s])
            total = total + both[:, 0:128] * donor_low[k] + both[:, 128:256] * donor_high[k]
        return total

    def applied():
        proj = dot(value[...].astype(BF16), mats_a[...])
        mid_l = (proj[:, 0:PADDED] * left_gain[...]).astype(BF16)
        mid_r = (proj[:, PADDED:] * right_gain[...]).astype(BF16)
        return dot(mid_l, mats_b[0:PADDED, :]) + dot(mid_r, mats_b[PADDED:, :])

    send_z(0, 1)
    for c in (1, 2):
        send_z(c, 0)
        send_z(c, 1)
    first_d()

    for c in (0, 1):
        state = unpack(c)
        own[0, :, 128 * c : 128 * c + 128] = value[:, 128 * c : 128 * c + 128].astype(BF16)
        send_donors(0, c)
        send_halo(0, c)
        gains(c, state)
    rest[:, 0:MAIN] = rhs_f[:, 0:MAIN] - faces_main(own_hot, own[0])
    state = unpack(2)
    stage_tail(0, 0, value[0:DONORS, MAIN:])
    send_donors(0, 2)
    stage_tail(0, 1, value[DONORS:, MAIN:])
    send_halo(0, 2)
    gains(2, state)
    received(0, 0)
    received(0, 1)
    rest[:, 0:MAIN] = rest[:, 0:MAIN] - faces_main(halo_hot, halo[0])
    received(0, 3)
    received(0, 4)
    rest[:, 0:MAIN] = rest[:, 0:MAIN] - fringe_main(0)
    rest[:, MAIN:] = rhs_f[:, MAIN:] - faces_tail(own_tail_hot, own_tail[0])
    rest[...] = rest[...] - applied()
    value[:, 0:MAIN] = rest[:, 0:MAIN] * inv_diag[:, 0:MAIN]
    own[1] = value[:, 0:MAIN].astype(BF16)
    for t in (0, 1):
        send_donors(1, t)
    for t in (0, 1):
        send_halo(1, t)
    rest[:, 0:MAIN] = rhs_f[:, 0:MAIN] - faces_main(own_hot, own[1])
    received(0, 2)
    turn(halo_tail, 0)
    rest[:, MAIN:] = rest[:, MAIN:] - faces_tail(halo_tail_hot, halo_tail[0])
    received(0, 5)
    value[:, MAIN:] = (rest[:, MAIN:] - fringe_tail(0)) * inv_diag[:, MAIN:]

    stage_tail(1, 0, value[0:DONORS, MAIN:])
    send_donors(1, 2)
    stage_tail(1, 1, value[DONORS:, MAIN:])
    send_halo(1, 2)
    rest[:, MAIN:] = rhs_f[:, MAIN:] - faces_tail(own_tail_hot, own_tail[1])
    rest[...] = rest[...] - applied()
    received(1, 0)
    received(1, 1)
    rest[:, 0:MAIN] = rest[:, 0:MAIN] - faces_main(halo_hot, halo[1])
    received(1, 3)
    received(1, 4)
    rest[:, 0:MAIN] = rest[:, 0:MAIN] - fringe_main(1)
    out[0:MAIN, :] = jnp.transpose(rest[:, 0:MAIN] * inv_diag[:, 0:MAIN])
    received(1, 2)
    turn(halo_tail, 1)
    rest[:, MAIN:] = rest[:, MAIN:] - faces_tail(halo_tail_hot, halo_tail[1])
    received(1, 5)
    last = (rest[:, MAIN:] - fringe_tail(1)) * inv_diag[:, MAIN:]
    out[MAIN:VALS, :] = jnp.transpose(last)[0 : VALS - MAIN, :]
    for c in range(3):
        arrived(send[c].at[sent_d if c else pl.ds(0, HALF - PART)], ds_sem.at[c])
        arrived(zpack[c].at[sent_z if c else half_rows], zs_sem.at[c])
    arrived(mid.at[half_sent], mid_sem.at[0])
    arrived(mid_pack.at[pl.ds(PART, HALF - PART)], mid_sem.at[2])
    for s in range(2):
        for n in range(6):
            arrived(moved_bytes(s, n), hs_sem.at[s, n])


def body(ckpt, rhs, npos, opos, lmat, rmat, fblk, fw, dblk, dw):
    args = (ckpt.T, rhs.T, npos.reshape(1, ROWS), opos.reshape(1, ROWS), lmat, rmat, fblk, fw, dblk, dw)
    dma = pltpu.SemaphoreType.DMA
    out = pl.pallas_call(
        kernel,
        out_shape=pltpu.VMEM((VALS, ROWS), F32),
        in_specs=[pl.BlockSpec(memory_space=pl.ANY)] * 10,
        out_specs=pl.BlockSpec(memory_space=pltpu.VMEM),
        scratch_shapes=[pltpu.VMEM(a.shape, a.dtype) for a in args]
        + [pltpu.VMEM((SLOTS, width), BF16) for _ in range(4) for width in WIDTHS]
        + [pltpu.VMEM((HALF, WIDTHS[0]), BF16)] * 2
        + [
            pltpu.VMEM((128, ROWS), F32),
            pltpu.VMEM((6 * ROWS, ROWS), BF16),
            pltpu.VMEM((6 * ROWS, DONORS), BF16),
            pltpu.VMEM((6 * ROWS, 2 * ROWS), BF16),
            pltpu.VMEM((6 * ROWS, 2 * DONORS), BF16),
            pltpu.VMEM((2 * ROWS, 3 * DONORS), BF16),
            pltpu.VMEM((2 * ROWS, 3 * 64), BF16),
            pltpu.VMEM((2, ROWS, MAIN), BF16),
            pltpu.VMEM((2, DONORS, 256), BF16),
            pltpu.VMEM((2, 2 * ROWS, MAIN), BF16),
            pltpu.VMEM((2, 2 * DONORS, 256), BF16),
            pltpu.VMEM((2, 3 * DONORS, MAIN), BF16),
            pltpu.VMEM((2, 3 * 64, 256), BF16),
            pltpu.VMEM((PADDED, 2 * PADDED), BF16),
            pltpu.VMEM((2 * PADDED, PADDED), BF16),
        ]
        + [pltpu.VMEM((6, ROWS, 128), F32)] * 3
        + [pltpu.VMEM((2, ROWS, 128), F32)] * 3
        + [pltpu.VMEM((ROWS, PADDED), F32)] * 6
        + [dma((len(args),))]
        + [dma((3,)), dma((3,)), dma((3,)), dma((3, 2)), dma((4,))]
        + [dma((2, 6))] * 2,
        compiler_params=pltpu.CompilerParams(collective_id=0, has_side_effects=True),
    )(*args)
    return out.T


def solution(mesh):
    row, vec, many = P(("blk", "grp"), None), P(("blk", "grp")), P(None, ("blk", "grp"))
    return jax.shard_map(
        body,
        mesh=mesh,
        in_specs=(row, row, vec, vec, P(), P(), many, many, many, many),
        out_specs=row,
        check_vma=False,
    )
```

```python
import jax
import jax.numpy as jnp
from jax import lax
from jax.experimental import pallas as pl
from jax.experimental.pallas import tpu as pltpu
from jax.sharding import PartitionSpec as P

MESH = pl.DeviceIdType.MESH
ROWS = 256
VALS = 320
MAIN = 256
PADDED = 384
BLK = 128
GRP = 4
NZ = 16
ND = 8
CAP = 4
SLOTS = BLK * CAP
DONORS = 128
PIECE = ND * CAP
HALF = SLOTS // 2
PART = HALF // ND
WIDTHS = (256, 256, 128)
F32 = jnp.float32
BF16 = jnp.bfloat16
ORDER = (0, 8, 9, 7, 10, 6, 11, 5, 12, 4, 13, 3, 15, 1, 14, 2)


def dot(a, b):
    return jnp.dot(a, b, preferred_element_type=F32)


def dot_t(a, b):
    return lax.dot_general(a, b, (((1,), (1,)), ((), ())), preferred_element_type=F32)


def iota(shape, dim):
    return lax.broadcasted_iota(jnp.int32, shape, dim)


def place_of(away):
    away = away & (NZ - 1)
    return sum(jnp.where(away == a, p, 0) for p, a in enumerate(ORDER) if p)


def arrived(ref, sem):
    pltpu.make_async_copy(ref, ref, sem).wait()


def remote(src, dst, send_sem, recv_sem, **where):
    return pltpu.make_async_remote_copy(
        src_ref=src, dst_ref=dst, send_sem=send_sem, recv_sem=recv_sem, device_id=where, device_id_type=MESH
    )


def kernel(
    ckpt_hbm, rhs_hbm, npos_hbm, opos_hbm, lmat_hbm, rmat_hbm, fblk_hbm, fw_hbm, dblk_hbm, dw_hbm, out,
    ckpt, rhs, npos, opos, lmat, rmat, fblk, fw, dblk, dw,
    send_0, send_1, send_2, dgot_0, dgot_1, dgot_2, zpack_0, zpack_1, zpack_2, got_0, got_1, got_2, mid, mid_pack, table,
    own_hot, own_tail_hot, halo_hot, halo_tail_hot, donor_hot, donor_tail_hot,
    own, own_tail, halo, halo_tail, donor_pool, donor_tail, mats_a, mats_b,
    face_scale, low_scale, high_scale, donor_scale, donor_low, donor_high,
    left_gain, right_gain, inv_diag, rhs_f, value, rest,
    in_sem, zs_sem, zr_sem, ds_sem, dr_sem, mid_sem, hs_sem, hr_sem,
):
    me = lax.axis_index("blk")
    grp = lax.axis_index("grp")
    my_z, my_d = me // ND, me % ND
    below, above = (me + BLK - 1) % BLK, (me + 1) % BLK

    send, dgot = (send_0, send_1, send_2), (dgot_0, dgot_1, dgot_2)
    zpack, got = (zpack_0, zpack_1, zpack_2), (got_0, got_1, got_2)

    barrier = pltpu.get_barrier_semaphore()

    def greet(**where):
        pl.semaphore_signal(barrier, inc=1, device_id=where, device_id_type=MESH)

    for away in (8, 7, 9, 6, 10, 5, 11, 4, 12, 3, 13, 2, 14, 1, 15):
        greet(blk=(my_z + away) % NZ * ND + my_d)
    for e in range(1, ND):
        greet(blk=my_z * ND + (my_d + e) % ND)
    for g in range(1, GRP):
        greet(grp=(grp + g) % GRP)
    greet(blk=below)
    greet(blk=above)

    pairs = (
        (npos_hbm, npos), (ckpt_hbm, ckpt), (rhs_hbm, rhs), (opos_hbm, opos), (fblk_hbm, fblk),
        (fw_hbm, fw), (dblk_hbm, dblk), (dw_hbm, dw), (lmat_hbm, lmat), (rmat_hbm, rmat),
    )
    loads = [pltpu.make_async_copy(a, b, in_sem.at[i]) for i, (a, b) in enumerate(pairs)]
    for load in loads:
        load.start()

    loads[0].wait()
    target = npos[...] >> 10
    key = place_of((target >> 3) - my_z) * ND + (((target & (ND - 1)) - my_d) & (ND - 1))
    hot = (key == iota((BLK, ROWS), 0)).astype(BF16)
    earlier = (iota((ROWS, ROWS), 0) < iota((ROWS, ROWS), 1)).astype(BF16)
    rank = jnp.sum(hot.astype(F32) * dot(hot, earlier), axis=0, keepdims=True)
    at = (key >> 6) * HALF + (key & (ND - 1)) * PART + ((key >> 3) & 7) * CAP
    slots = iota((SLOTS, ROWS), 0).astype(F32)
    put = (at.astype(F32) + rank == slots).astype(BF16)
    at = jnp.where(key < BLK // 2, key * CAP, at)
    put_first = (at.astype(F32) + rank == slots).astype(BF16)
    loads[1].wait()
    loads[2].wait()

    def pack(c):
        last = c == 2
        count = VALS - MAIN if last else 128
        at = slice(128 * c, 128 * c + count)
        both = jnp.concatenate([ckpt[at, :], rhs[at, :]], axis=0)
        send[c][...] = dot_t(put if c else put_first, both).astype(BF16)

    def send_d(c):
        for h in range(2) if c else (1,):
            for e in (4, 5, 3, 2, 6, 7, 1):
                part = pl.ds(h * HALF + e * PART, PART)
                to = my_z * ND + (my_d + e) % ND
                remote(send[c].at[part], dgot[c].at[part], ds_sem.at[c], dr_sem.at[c, h], blk=to).start()
            kept = slice(h * HALF, h * HALF + PART)
            dgot[c][kept, :] = send[c][kept, :]

    row, col = iota((HALF, HALF), 0), iota((HALF, HALF), 1)
    regroup = (col == ((row // CAP) % ND) * PART + (row // PIECE) * CAP + row % CAP).astype(BF16)
    sent_z, sent_d = pl.ds(PIECE, SLOTS - PIECE), pl.ds(2 * PART, SLOTS - 2 * PART)

    def send_z(c, h):
        arrived(dgot[c].at[pl.ds(0, HALF - PART)], dr_sem.at[c, h])
        rows = slice(h * HALF, (h + 1) * HALF)
        moved = dot(regroup, dgot[c][rows, :]).astype(BF16)
        zpack[c][rows, :] = moved
        for p in range(8 * h, 8 * h + 8):
            if p:
                part = pl.ds(p * PIECE, PIECE)
                to = (my_z + ORDER[p]) % NZ * ND + my_d
                remote(zpack[c].at[part], got[c].at[part], zs_sem.at[c], zr_sem.at[c], blk=to).start()
        if h == 0:
            got[c][0:PIECE, :] = moved[0:PIECE, :]

    half_rows, half_sent = pl.ds(HALF, HALF), pl.ds(PIECE, HALF - PIECE)

    def first_z():
        for p in range(1, 8):
            part = pl.ds(p * PIECE, PIECE)
            to = (my_z + ORDER[p]) % NZ * ND + my_d
            remote(send[0].at[part], mid.at[part], mid_sem.at[0], mid_sem.at[1], blk=to).start()
        mid[0:PIECE, :] = send[0][0:PIECE, :]

    def first_d():
        arrived(mid.at[half_sent], mid_sem.at[1])
        back = (col == ((row // CAP) % ND) * PIECE + (row // PART) * CAP + row % CAP).astype(BF16)
        moved = dot(back, mid[...]).astype(BF16)
        mid_pack[...] = moved
        for e in (4, 5, 3, 2, 6, 7, 1):
            part = pl.ds(e * PART, PART)
            to = my_z * ND + (my_d + e) % ND
            remote(mid_pack.at[part], got[0].at[part], mid_sem.at[2], mid_sem.at[3], blk=to).start()
        got[0][0:PART, :] = moved[0:PART, :]

    pack(0)
    pl.semaphore_wait(barrier, NZ - 1 + ND - 1 + GRP - 1 + 2)
    first_z()
    send_d(0)
    for c in (1, 2):
        pack(c)
        send_d(c)

    for load in loads[3:]:
        load.wait()
    table[...] = jnp.zeros_like(table)
    faces = fblk[...]
    side = jnp.where(faces >= 0, ((faces >> 10) - me + 1) & (BLK - 1), -1)
    local = faces & (ROWS - 1)
    packed = ((local >> 7) << 6) + (local & 63)
    away_side = (side >> 1) & 1
    outer = (side == 0) | (side == 2)
    table[0:6, :] = jnp.where(outer, away_side * ROWS + local, -1).astype(F32)
    table[8:14, :] = fw[...]
    table[48:54, :] = jnp.where(side == 1, local, -1).astype(F32)
    table[56:62, :] = jnp.where(outer, away_side * DONORS + packed, -1).astype(F32)
    table[64:70, :] = jnp.where(side == 1, packed, -1).astype(F32)
    table[72:78, :] = ((local >> 6) & 1).astype(F32)
    donors = dblk[...]
    donor_grp = (((donors >> 8) - grp) & (GRP - 1)) - 1
    table[16:18, :] = (donor_grp * DONORS + (donors & (DONORS - 1))).astype(F32)
    table[80:82, :] = (donor_grp * 64 + (donors & 63)).astype(F32)
    table[88:90, :] = ((donors >> 6) & 1).astype(F32)
    table[24:26, :] = dw[...]
    anchor = opos[...] >> 10
    e = (my_d - (anchor & (ND - 1))) & (ND - 1)
    place = place_of(my_z - (anchor >> 3))
    order_row = ((place * ND + e) * ROWS + (opos[...] & (ROWS - 1))).astype(F32)
    base = place * PIECE + e * CAP
    table[32:33, :] = order_row
    table[40:41, :] = base.astype(F32)
    table[41:42, :] = jnp.where(place < ND, e * PART + place * CAP, base).astype(F32)
    columns = jnp.transpose(table[...])

    def column(n):
        return columns[:, n : n + 1]

    smaller = (order_row < column(32)).astype(BF16)
    rank = dot(smaller, jnp.ones((ROWS, 128), BF16)).astype(jnp.int32) & (CAP - 1)
    lanes = iota((ROWS, 128), 1).astype(F32)

    def picks(n):
        recv_slot = rank.astype(F32) + column(n)
        return jnp.concatenate(
            [(recv_slot == lanes + 128.0 * t).astype(BF16) for t in range(SLOTS // 128)], axis=1
        )

    pick, pick_first = picks(40), picks(41)

    def select(ref, first, count):
        lane = iota((ROWS, ref.shape[1]), 1).astype(F32)
        for n in range(count):
            ref[n * ROWS : (n + 1) * ROWS, :] = (column(first + n) == lane).astype(BF16)

    select(halo_hot, 0, 6)
    select(own_hot, 48, 6)
    select(halo_tail_hot, 56, 6)
    select(own_tail_hot, 64, 6)
    select(donor_hot, 16, 2)
    select(donor_tail_hot, 80, 2)

    lane = iota((ROWS, 128), 1)
    for f in range(6):
        cell = lane // (16, 4, 1)[f // 2] % 4
        scale = jnp.where(cell == (3 if f % 2 == 0 else 0), column(8 + f), 0.0)
        face_scale[f] = scale
        high = jnp.broadcast_to(column(72 + f), (ROWS, 128))
        low_scale[f] = jnp.where(high > 0.5, 0.0, scale)
        high_scale[f] = jnp.where(high > 0.5, scale, 0.0)
    for k in range(2):
        scale = jnp.broadcast_to(column(24 + k), (ROWS, 128))
        donor_scale[k] = scale
        high = jnp.broadcast_to(column(88 + k), (ROWS, 128))
        donor_low[k] = jnp.where(high > 0.5, 0.0, scale)
        donor_high[k] = jnp.where(high > 0.5, scale, 0.0)

    mats_a[...] = jnp.zeros_like(mats_a)
    mats_b[...] = jnp.zeros_like(mats_b)
    mats_a[0:VALS, 0:VALS] = lmat[...]
    mats_b[0:VALS, 0:VALS] = rmat[...]
    mats_a[:, PADDED:] = jnp.transpose(mats_b[0:PADDED, :])
    mats_b[PADDED:, :] = jnp.transpose(mats_a[:, 0:PADDED])

    half = iota((ROWS, 128), 1) < 64

    def unpack(c):
        arrived(got[c].at[sent_z if c else half_rows], zr_sem.at[c])
        if c == 0:
            arrived(got[0].at[pl.ds(PART, HALF - PART)], mid_sem.at[3])
        both = dot(pick if c else pick_first, got[c][...])
        if c == 2:
            state = jnp.where(half, both, 0.0)
            right_side = jnp.where(half, pltpu.roll(both, 64, 1), 0.0)
        else:
            state, right_side = both[:, 0:128], both[:, 128:256]
        at = slice(128 * c, 128 * c + 128)
        diag = 1.0 / (2.0 + state * state)
        inv_diag[:, at] = diag
        rhs_f[:, at] = right_side
        value[:, at] = right_side * diag
        return state

    def gains(c, state):
        at = slice(128 * c, 128 * c + 128)
        left_gain[:, at] = 0.5 * jnp.tanh(state)
        right_gain[:, at] = 0.4 * jnp.tanh(1.5 * state - 0.5)

    def stage_tail(s, h, tails):
        low, high = tails[0:64], tails[64:128]
        turned_low, turned_high = pltpu.roll(low, 64, 1), pltpu.roll(high, 64, 1)
        at = slice(64 * h, 64 * h + 64)
        own_tail[s, at, 0:128] = jnp.where(half[0:64], low, turned_high).astype(BF16)
        own_tail[s, at, 128:256] = jnp.where(half[0:64], high, turned_low).astype(BF16)

    def turn(ref, s):
        ref[s, :, 128:256] = pltpu.roll(ref[s, :, 0:128].astype(F32), 64, 1).astype(BF16)

    def lanes_of(t):
        return pl.ds(128 if t == 1 else 0, 128)

    def send_donors(s, t):
        src, dst, rows = (own_tail, donor_tail, 64) if t == 2 else (own, donor_pool, DONORS)
        for g in (2, 1, 3):
            remote(
                src.at[s, pl.ds(0, rows), lanes_of(t)],
                dst.at[s, pl.ds((g - 1) * rows, rows), lanes_of(t)],
                hs_sem.at[s, 3 + t], hr_sem.at[s, 3 + t], grp=(grp + GRP - g) % GRP,
            ).start()

    def send_halo(s, t):
        src, dst, rows = (own_tail, halo_tail, DONORS) if t == 2 else (own, halo, ROWS)
        for n, to in enumerate((above, below)):
            remote(
                src.at[s, :, lanes_of(t)], dst.at[s, pl.ds(n * rows, rows), lanes_of(t)],
                hs_sem.at[s, t], hr_sem.at[s, t], blk=to,
            ).start()

    def moved_bytes(s, n):
        ref = (halo, halo, halo_tail, donor_pool, donor_pool, donor_tail)[n]
        return ref.at[s, :, lanes_of(n % 3)]

    def received(s, n):
        arrived(moved_bytes(s, n), hr_sem.at[s, n])

    def placed(f, part):
        stride = (16, 4, 1)[f // 2]
        return pltpu.roll(part, 128 - 3 * stride if f % 2 == 0 else 3 * stride, 1)

    def faces_main(hot, rows_of):
        tiles = [jnp.zeros((ROWS, 128), F32) for _ in range(2)]
        for f in range(6):
            fetched = dot(hot[f * ROWS : (f + 1) * ROWS, :], rows_of)
            scale = face_scale[f]
            tiles = [tiles[t] + placed(f, fetched[:, 128 * t : 128 * t + 128] * scale) for t in range(2)]
        return jnp.concatenate(tiles, axis=1)

    def faces_tail(hot, rows_of):
        total = jnp.zeros((ROWS, 128), F32)
        for f in range(6):
            both = dot(hot[f * ROWS : (f + 1) * ROWS, :], rows_of)
            total = total + placed(f, both[:, 0:128] * low_scale[f] + both[:, 128:256] * high_scale[f])
        return total

    def fringe_main(s):
        total = [jnp.zeros((ROWS, 128), F32) for _ in range(2)]
        for k in range(2):
            fetched = dot(donor_hot[k * ROWS : (k + 1) * ROWS, :], donor_pool[s])
            scale = donor_scale[k]
            total = [total[t] + fetched[:, 128 * t : 128 * t + 128] * scale for t in range(2)]
        return jnp.concatenate(total, axis=1)

    def fringe_tail(s):
        turn(donor_tail, s)
        total = jnp.zeros((ROWS, 128), F32)
        for k in range(2):
            both = dot(donor_tail_hot[k * ROWS : (k + 1) * ROWS, :], donor_tail[s])
            total = total + both[:, 0:128] * donor_low[k] + both[:, 128:256] * donor_high[k]
        return total

    def applied():
        proj = dot(value[...].astype(BF16), mats_a[...])
        mid_l = (proj[:, 0:PADDED] * left_gain[...]).astype(BF16)
        mid_r = (proj[:, PADDED:] * right_gain[...]).astype(BF16)
        return dot(mid_l, mats_b[0:PADDED, :]) + dot(mid_r, mats_b[PADDED:, :])

    send_z(0, 1)
    for c in (1, 2):
        send_z(c, 0)
        send_z(c, 1)
    first_d()

    for c in (0, 1):
        state = unpack(c)
        own[0, :, 128 * c : 128 * c + 128] = value[:, 128 * c : 128 * c + 128].astype(BF16)
        send_donors(0, c)
        send_halo(0, c)
        gains(c, state)
    rest[:, 0:MAIN] = rhs_f[:, 0:MAIN] - faces_main(own_hot, own[0])
    state = unpack(2)
    stage_tail(0, 0, value[0:DONORS, MAIN:])
    send_donors(0, 2)
    stage_tail(0, 1, value[DONORS:, MAIN:])
    send_halo(0, 2)
    gains(2, state)
    rest[:, MAIN:] = rhs_f[:, MAIN:] - faces_tail(own_tail_hot, own_tail[0])
    rest[...] = rest[...] - applied()
    received(0, 0)
    received(0, 1)
    rest[:, 0:MAIN] = rest[:, 0:MAIN] - faces_main(halo_hot, halo[0])
    received(0, 3)
    received(0, 4)
    rest[:, 0:MAIN] = rest[:, 0:MAIN] - fringe_main(0)
    value[:, 0:MAIN] = rest[:, 0:MAIN] * inv_diag[:, 0:MAIN]
    own[1] = value[:, 0:MAIN].astype(BF16)
    for t in (0, 1):
        send_donors(1, t)
    for t in (0, 1):
        send_halo(1, t)
    received(0, 2)
    turn(halo_tail, 0)
    rest[:, MAIN:] = rest[:, MAIN:] - faces_tail(halo_tail_hot, halo_tail[0])
    received(0, 5)
    value[:, MAIN:] = (rest[:, MAIN:] - fringe_tail(0)) * inv_diag[:, MAIN:]

    stage_tail(1, 0, value[0:DONORS, MAIN:])
    send_donors(1, 2)
    stage_tail(1, 1, value[DONORS:, MAIN:])
    send_halo(1, 2)
    rest[:, 0:MAIN] = rhs_f[:, 0:MAIN] - faces_main(own_hot, own[1])
    rest[:, MAIN:] = rhs_f[:, MAIN:] - faces_tail(own_tail_hot, own_tail[1])
    rest[...] = rest[...] - applied()
    received(1, 0)
    received(1, 1)
    rest[:, 0:MAIN] = rest[:, 0:MAIN] - faces_main(halo_hot, halo[1])
    received(1, 2)
    turn(halo_tail, 1)
    rest[:, MAIN:] = rest[:, MAIN:] - faces_tail(halo_tail_hot, halo_tail[1])
    received(1, 3)
    received(1, 4)
    rest[:, 0:MAIN] = rest[:, 0:MAIN] - fringe_main(1)
    out[0:MAIN, :] = jnp.transpose(rest[:, 0:MAIN] * inv_diag[:, 0:MAIN])
    received(1, 5)
    last = (rest[:, MAIN:] - fringe_tail(1)) * inv_diag[:, MAIN:]
    out[MAIN:VALS, :] = jnp.transpose(last)[0 : VALS - MAIN, :]
    for c in range(3):
        arrived(send[c].at[sent_d if c else pl.ds(0, HALF - PART)], ds_sem.at[c])
        arrived(zpack[c].at[sent_z if c else half_rows], zs_sem.at[c])
    arrived(mid.at[half_sent], mid_sem.at[0])
    arrived(mid_pack.at[pl.ds(PART, HALF - PART)], mid_sem.at[2])
    for s in range(2):
        for n in range(6):
            arrived(moved_bytes(s, n), hs_sem.at[s, n])


def body(ckpt, rhs, npos, opos, lmat, rmat, fblk, fw, dblk, dw):
    args = (ckpt.T, rhs.T, npos.reshape(1, ROWS), opos.reshape(1, ROWS), lmat, rmat, fblk, fw, dblk, dw)
    dma = pltpu.SemaphoreType.DMA
    out = pl.pallas_call(
        kernel,
        out_shape=pltpu.VMEM((VALS, ROWS), F32),
        in_specs=[pl.BlockSpec(memory_space=pl.ANY)] * 10,
        out_specs=pl.BlockSpec(memory_space=pltpu.VMEM),
        scratch_shapes=[pltpu.VMEM(a.shape, a.dtype) for a in args]
        + [pltpu.VMEM((SLOTS, width), BF16) for _ in range(4) for width in WIDTHS]
        + [pltpu.VMEM((HALF, WIDTHS[0]), BF16)] * 2
        + [
            pltpu.VMEM((128, ROWS), F32),
            pltpu.VMEM((6 * ROWS, ROWS), BF16),
            pltpu.VMEM((6 * ROWS, DONORS), BF16),
            pltpu.VMEM((6 * ROWS, 2 * ROWS), BF16),
            pltpu.VMEM((6 * ROWS, 2 * DONORS), BF16),
            pltpu.VMEM((2 * ROWS, 3 * DONORS), BF16),
            pltpu.VMEM((2 * ROWS, 3 * 64), BF16),
            pltpu.VMEM((2, ROWS, MAIN), BF16),
            pltpu.VMEM((2, DONORS, 256), BF16),
            pltpu.VMEM((2, 2 * ROWS, MAIN), BF16),
            pltpu.VMEM((2, 2 * DONORS, 256), BF16),
            pltpu.VMEM((2, 3 * DONORS, MAIN), BF16),
            pltpu.VMEM((2, 3 * 64, 256), BF16),
            pltpu.VMEM((PADDED, 2 * PADDED), BF16),
            pltpu.VMEM((2 * PADDED, PADDED), BF16),
        ]
        + [pltpu.VMEM((6, ROWS, 128), F32)] * 3
        + [pltpu.VMEM((2, ROWS, 128), F32)] * 3
        + [pltpu.VMEM((ROWS, PADDED), F32)] * 6
        + [dma((len(args),))]
        + [dma((3,)), dma((3,)), dma((3,)), dma((3, 2)), dma((4,))]
        + [dma((2, 6))] * 2,
        compiler_params=pltpu.CompilerParams(collective_id=0, has_side_effects=True),
    )(*args)
    return out.T


def solution(mesh):
    row, vec, many = P(("blk", "grp"), None), P(("blk", "grp")), P(None, ("blk", "grp"))
    return jax.shard_map(
        body,
        mesh=mesh,
        in_specs=(row, row, vec, vec, P(), P(), many, many, many, many),
        out_specs=row,
        check_vma=False,
    )
```

```python
import jax
import jax.numpy as jnp
from jax import lax
from jax.experimental import pallas as pl
from jax.experimental.pallas import tpu as pltpu
from jax.sharding import PartitionSpec as P

MESH = pl.DeviceIdType.MESH
ROWS = 256
VALS = 320
MAIN = 256
PADDED = 384
BLK = 128
GRP = 4
NZ = 16
ND = 8
CAP = 4
SLOTS = BLK * CAP
DONORS = 128
PIECE = ND * CAP
HALF = SLOTS // 2
PART = HALF // ND
WIDTHS = (256, 256, 128)
F32 = jnp.float32
BF16 = jnp.bfloat16
ORDER = (0, 8, 9, 7, 10, 6, 11, 5, 12, 4, 13, 3, 15, 1, 14, 2)


def dot(a, b):
    return jnp.dot(a, b, preferred_element_type=F32)


def dot_t(a, b):
    return lax.dot_general(a, b, (((1,), (1,)), ((), ())), preferred_element_type=F32)


def iota(shape, dim):
    return lax.broadcasted_iota(jnp.int32, shape, dim)


def place_of(away):
    away = away & (NZ - 1)
    return sum(jnp.where(away == a, p, 0) for p, a in enumerate(ORDER) if p)


def arrived(ref, sem):
    pltpu.make_async_copy(ref, ref, sem).wait()


def remote(src, dst, send_sem, recv_sem, **where):
    return pltpu.make_async_remote_copy(
        src_ref=src, dst_ref=dst, send_sem=send_sem, recv_sem=recv_sem, device_id=where, device_id_type=MESH
    )


def kernel(
    ckpt_hbm, rhs_hbm, npos_hbm, opos_hbm, lmat_hbm, rmat_hbm, fblk_hbm, fw_hbm, dblk_hbm, dw_hbm, out,
    ckpt, rhs, npos, opos, lmat, rmat, fblk, fw, dblk, dw,
    send_0, send_1, send_2, dgot_0, dgot_1, dgot_2, zpack_0, zpack_1, zpack_2, got_0, got_1, got_2, mid, mid_pack, table,
    own_hot, own_tail_hot, halo_hot, halo_tail_hot, donor_hot, donor_tail_hot,
    own, own_tail, halo, halo_tail, donor_pool, donor_tail, mats_a, mats_b,
    face_scale, low_scale, high_scale, donor_scale, donor_low, donor_high,
    left_gain, right_gain, inv_diag, rhs_f, value, rest,
    in_sem, zs_sem, zr_sem, ds_sem, dr_sem, mid_sem, hs_sem, hr_sem,
):
    me = lax.axis_index("blk")
    grp = lax.axis_index("grp")
    my_z, my_d = me // ND, me % ND
    below, above = (me + BLK - 1) % BLK, (me + 1) % BLK

    send, dgot = (send_0, send_1, send_2), (dgot_0, dgot_1, dgot_2)
    zpack, got = (zpack_0, zpack_1, zpack_2), (got_0, got_1, got_2)

    barrier = pltpu.get_barrier_semaphore()

    def greet(**where):
        pl.semaphore_signal(barrier, inc=1, device_id=where, device_id_type=MESH)

    pairs = (
        (npos_hbm, npos), (ckpt_hbm, ckpt), (rhs_hbm, rhs), (opos_hbm, opos), (fblk_hbm, fblk),
        (fw_hbm, fw), (dblk_hbm, dblk), (dw_hbm, dw), (lmat_hbm, lmat), (rmat_hbm, rmat),
    )
    loads = [pltpu.make_async_copy(a, b, in_sem.at[i]) for i, (a, b) in enumerate(pairs)]
    for load in loads:
        load.start()

    for away in (8, 7, 9, 6, 10, 5, 11, 4, 12, 3, 13, 2, 14, 1, 15):
        greet(blk=(my_z + away) % NZ * ND + my_d)
    for e in range(1, ND):
        greet(blk=my_z * ND + (my_d + e) % ND)
    for g in range(1, GRP):
        greet(grp=(grp + g) % GRP)
    greet(blk=below)
    greet(blk=above)

    loads[0].wait()
    target = npos[...] >> 10
    key = place_of((target >> 3) - my_z) * ND + (((target & (ND - 1)) - my_d) & (ND - 1))
    hot = (key == iota((BLK, ROWS), 0)).astype(BF16)
    earlier = (iota((ROWS, ROWS), 0) < iota((ROWS, ROWS), 1)).astype(BF16)
    rank = jnp.sum(hot.astype(F32) * dot(hot, earlier), axis=0, keepdims=True)
    at = (key >> 6) * HALF + (key & (ND - 1)) * PART + ((key >> 3) & 7) * CAP
    slots = iota((SLOTS, ROWS), 0).astype(F32)
    put = (at.astype(F32) + rank == slots).astype(BF16)
    at = jnp.where(key < BLK // 2, key * CAP, at)
    put_first = (at.astype(F32) + rank == slots).astype(BF16)
    loads[1].wait()
    loads[2].wait()

    def pack(c):
        last = c == 2
        count = VALS - MAIN if last else 128
        at = slice(128 * c, 128 * c + count)
        both = jnp.concatenate([ckpt[at, :], rhs[at, :]], axis=0)
        send[c][...] = dot_t(put if c else put_first, both).astype(BF16)

    def send_d(c):
        for h in range(2) if c else (1,):
            for e in (4, 5, 3, 2, 6, 7, 1):
                part = pl.ds(h * HALF + e * PART, PART)
                to = my_z * ND + (my_d + e) % ND
                remote(send[c].at[part], dgot[c].at[part], ds_sem.at[c], dr_sem.at[c, h], blk=to).start()
            kept = slice(h * HALF, h * HALF + PART)
            dgot[c][kept, :] = send[c][kept, :]

    row, col = iota((HALF, HALF), 0), iota((HALF, HALF), 1)
    regroup = (col == ((row // CAP) % ND) * PART + (row // PIECE) * CAP + row % CAP).astype(BF16)
    sent_z, sent_d = pl.ds(PIECE, SLOTS - PIECE), pl.ds(2 * PART, SLOTS - 2 * PART)

    def send_z(c, h):
        arrived(dgot[c].at[pl.ds(0, HALF - PART)], dr_sem.at[c, h])
        rows = slice(h * HALF, (h + 1) * HALF)
        moved = dot(regroup, dgot[c][rows, :]).astype(BF16)
        zpack[c][rows, :] = moved
        for p in range(8 * h, 8 * h + 8):
            if p:
                part = pl.ds(p * PIECE, PIECE)
                to = (my_z + ORDER[p]) % NZ * ND + my_d
                remote(zpack[c].at[part], got[c].at[part], zs_sem.at[c], zr_sem.at[c], blk=to).start()
        if h == 0:
            got[c][0:PIECE, :] = moved[0:PIECE, :]

    half_rows, half_sent = pl.ds(HALF, HALF), pl.ds(PIECE, HALF - PIECE)

    def first_z():
        for p in range(1, 8):
            part = pl.ds(p * PIECE, PIECE)
            to = (my_z + ORDER[p]) % NZ * ND + my_d
            remote(send[0].at[part], mid.at[part], mid_sem.at[0], mid_sem.at[1], blk=to).start()
        mid[0:PIECE, :] = send[0][0:PIECE, :]

    def first_d():
        arrived(mid.at[half_sent], mid_sem.at[1])
        back = (col == ((row // CAP) % ND) * PIECE + (row // PART) * CAP + row % CAP).astype(BF16)
        moved = dot(back, mid[...]).astype(BF16)
        mid_pack[...] = moved
        for e in (4, 5, 3, 2, 6, 7, 1):
            part = pl.ds(e * PART, PART)
            to = my_z * ND + (my_d + e) % ND
            remote(mid_pack.at[part], got[0].at[part], mid_sem.at[2], mid_sem.at[3], blk=to).start()
        got[0][0:PART, :] = moved[0:PART, :]

    pack(0)
    pl.semaphore_wait(barrier, NZ - 1 + ND - 1 + GRP - 1 + 2)
    first_z()
    send_d(0)
    for c in (1, 2):
        pack(c)
        send_d(c)

    for load in loads[3:]:
        load.wait()
    table[...] = jnp.zeros_like(table)
    faces = fblk[...]
    side = jnp.where(faces >= 0, ((faces >> 10) - me + 1) & (BLK - 1), -1)
    local = faces & (ROWS - 1)
    packed = ((local >> 7) << 6) + (local & 63)
    away_side = (side >> 1) & 1
    outer = (side == 0) | (side == 2)
    table[0:6, :] = jnp.where(outer, away_side * ROWS + local, -1).astype(F32)
    table[8:14, :] = fw[...]
    table[48:54, :] = jnp.where(side == 1, local, -1).astype(F32)
    table[56:62, :] = jnp.where(outer, away_side * DONORS + packed, -1).astype(F32)
    table[64:70, :] = jnp.where(side == 1, packed, -1).astype(F32)
    table[72:78, :] = ((local >> 6) & 1).astype(F32)
    donors = dblk[...]
    donor_grp = (((donors >> 8) - grp) & (GRP - 1)) - 1
    table[16:18, :] = (donor_grp * DONORS + (donors & (DONORS - 1))).astype(F32)
    table[80:82, :] = (donor_grp * 64 + (donors & 63)).astype(F32)
    table[88:90, :] = ((donors >> 6) & 1).astype(F32)
    table[24:26, :] = dw[...]
    anchor = opos[...] >> 10
    e = (my_d - (anchor & (ND - 1))) & (ND - 1)
    place = place_of(my_z - (anchor >> 3))
    order_row = ((place * ND + e) * ROWS + (opos[...] & (ROWS - 1))).astype(F32)
    base = place * PIECE + e * CAP
    table[32:33, :] = order_row
    table[40:41, :] = base.astype(F32)
    table[41:42, :] = jnp.where(place < ND, e * PART + place * CAP, base).astype(F32)
    columns = jnp.transpose(table[...])

    def column(n):
        return columns[:, n : n + 1]

    smaller = (order_row < column(32)).astype(BF16)
    rank = dot(smaller, jnp.ones((ROWS, 128), BF16)).astype(jnp.int32) & (CAP - 1)
    lanes = iota((ROWS, 128), 1).astype(F32)

    def picks(n):
        recv_slot = rank.astype(F32) + column(n)
        return jnp.concatenate(
            [(recv_slot == lanes + 128.0 * t).astype(BF16) for t in range(SLOTS // 128)], axis=1
        )

    pick, pick_first = picks(40), picks(41)

    def select(ref, first, count):
        lane = iota((ROWS, ref.shape[1]), 1).astype(F32)
        for n in range(count):
            ref[n * ROWS : (n + 1) * ROWS, :] = (column(first + n) == lane).astype(BF16)

    select(halo_hot, 0, 6)
    select(own_hot, 48, 6)
    select(halo_tail_hot, 56, 6)
    select(own_tail_hot, 64, 6)
    select(donor_hot, 16, 2)
    select(donor_tail_hot, 80, 2)

    lane = iota((ROWS, 128), 1)
    for f in range(6):
        cell = lane // (16, 4, 1)[f // 2] % 4
        scale = jnp.where(cell == (3 if f % 2 == 0 else 0), column(8 + f), 0.0)
        face_scale[f] = scale
        high = jnp.broadcast_to(column(72 + f), (ROWS, 128))
        low_scale[f] = jnp.where(high > 0.5, 0.0, scale)
        high_scale[f] = jnp.where(high > 0.5, scale, 0.0)
    for k in range(2):
        scale = jnp.broadcast_to(column(24 + k), (ROWS, 128))
        donor_scale[k] = scale
        high = jnp.broadcast_to(column(88 + k), (ROWS, 128))
        donor_low[k] = jnp.where(high > 0.5, 0.0, scale)
        donor_high[k] = jnp.where(high > 0.5, scale, 0.0)

    mats_a[...] = jnp.zeros_like(mats_a)
    mats_b[...] = jnp.zeros_like(mats_b)
    mats_a[0:VALS, 0:VALS] = lmat[...]
    mats_b[0:VALS, 0:VALS] = rmat[...]
    mats_a[:, PADDED:] = jnp.transpose(mats_b[0:PADDED, :])
    mats_b[PADDED:, :] = jnp.transpose(mats_a[:, 0:PADDED])

    half = iota((ROWS, 128), 1) < 64

    def unpack(c):
        arrived(got[c].at[sent_z if c else half_rows], zr_sem.at[c])
        if c == 0:
            arrived(got[0].at[pl.ds(PART, HALF - PART)], mid_sem.at[3])
        both = dot(pick if c else pick_first, got[c][...])
        if c == 2:
            state = jnp.where(half, both, 0.0)
            right_side = jnp.where(half, pltpu.roll(both, 64, 1), 0.0)
        else:
            state, right_side = both[:, 0:128], both[:, 128:256]
        at = slice(128 * c, 128 * c + 128)
        diag = 1.0 / (2.0 + state * state)
        inv_diag[:, at] = diag
        rhs_f[:, at] = right_side
        value[:, at] = right_side * diag
        return state

    def gains(c, state):
        at = slice(128 * c, 128 * c + 128)
        left_gain[:, at] = 0.5 * jnp.tanh(state)
        right_gain[:, at] = 0.4 * jnp.tanh(1.5 * state - 0.5)

    def stage_tail(s, h, tails):
        low, high = tails[0:64], tails[64:128]
        turned_low, turned_high = pltpu.roll(low, 64, 1), pltpu.roll(high, 64, 1)
        at = slice(64 * h, 64 * h + 64)
        own_tail[s, at, 0:128] = jnp.where(half[0:64], low, turned_high).astype(BF16)
        own_tail[s, at, 128:256] = jnp.where(half[0:64], high, turned_low).astype(BF16)

    def turn(ref, s):
        ref[s, :, 128:256] = pltpu.roll(ref[s, :, 0:128].astype(F32), 64, 1).astype(BF16)

    def lanes_of(t):
        return pl.ds(128 if t == 1 else 0, 128)

    def send_donors(s, t):
        src, dst, rows = (own_tail, donor_tail, 64) if t == 2 else (own, donor_pool, DONORS)
        for g in (2, 1, 3):
            remote(
                src.at[s, pl.ds(0, rows), lanes_of(t)],
                dst.at[s, pl.ds((g - 1) * rows, rows), lanes_of(t)],
                hs_sem.at[s, 3 + t], hr_sem.at[s, 3 + t], grp=(grp + GRP - g) % GRP,
            ).start()

    def send_halo(s, t):
        src, dst, rows = (own_tail, halo_tail, DONORS) if t == 2 else (own, halo, ROWS)
        for n, to in enumerate((above, below)):
            remote(
                src.at[s, :, lanes_of(t)], dst.at[s, pl.ds(n * rows, rows), lanes_of(t)],
                hs_sem.at[s, t], hr_sem.at[s, t], blk=to,
            ).start()

    def moved_bytes(s, n):
        ref = (halo, halo, halo_tail, donor_pool, donor_pool, donor_tail)[n]
        return ref.at[s, :, lanes_of(n % 3)]

    def received(s, n):
        arrived(moved_bytes(s, n), hr_sem.at[s, n])

    def placed(f, part):
        stride = (16, 4, 1)[f // 2]
        return pltpu.roll(part, 128 - 3 * stride if f % 2 == 0 else 3 * stride, 1)

    def faces_main(hot, rows_of):
        tiles = [jnp.zeros((ROWS, 128), F32) for _ in range(2)]
        for f in range(6):
            fetched = dot(hot[f * ROWS : (f + 1) * ROWS, :], rows_of)
            scale = face_scale[f]
            tiles = [tiles[t] + placed(f, fetched[:, 128 * t : 128 * t + 128] * scale) for t in range(2)]
        return jnp.concatenate(tiles, axis=1)

    def faces_tail(hot, rows_of):
        total = jnp.zeros((ROWS, 128), F32)
        for f in range(6):
            both = dot(hot[f * ROWS : (f + 1) * ROWS, :], rows_of)
            total = total + placed(f, both[:, 0:128] * low_scale[f] + both[:, 128:256] * high_scale[f])
        return total

    def fringe_main(s):
        total = [jnp.zeros((ROWS, 128), F32) for _ in range(2)]
        for k in range(2):
            fetched = dot(donor_hot[k * ROWS : (k + 1) * ROWS, :], donor_pool[s])
            scale = donor_scale[k]
            total = [total[t] + fetched[:, 128 * t : 128 * t + 128] * scale for t in range(2)]
        return jnp.concatenate(total, axis=1)

    def fringe_tail(s):
        turn(donor_tail, s)
        total = jnp.zeros((ROWS, 128), F32)
        for k in range(2):
            both = dot(donor_tail_hot[k * ROWS : (k + 1) * ROWS, :], donor_tail[s])
            total = total + both[:, 0:128] * donor_low[k] + both[:, 128:256] * donor_high[k]
        return total

    def applied():
        proj = dot(value[...].astype(BF16), mats_a[...])
        mid_l = (proj[:, 0:PADDED] * left_gain[...]).astype(BF16)
        mid_r = (proj[:, PADDED:] * right_gain[...]).astype(BF16)
        return dot(mid_l, mats_b[0:PADDED, :]) + dot(mid_r, mats_b[PADDED:, :])

    send_z(0, 1)
    for c in (1, 2):
        send_z(c, 0)
        send_z(c, 1)
    first_d()

    for c in (0, 1):
        state = unpack(c)
        own[0, :, 128 * c : 128 * c + 128] = value[:, 128 * c : 128 * c + 128].astype(BF16)
        send_donors(0, c)
        send_halo(0, c)
        gains(c, state)
    rest[:, 0:MAIN] = rhs_f[:, 0:MAIN] - faces_main(own_hot, own[0])
    state = unpack(2)
    stage_tail(0, 0, value[0:DONORS, MAIN:])
    send_donors(0, 2)
    stage_tail(0, 1, value[DONORS:, MAIN:])
    send_halo(0, 2)
    gains(2, state)
    rest[:, MAIN:] = rhs_f[:, MAIN:] - faces_tail(own_tail_hot, own_tail[0])
    rest[...] = rest[...] - applied()
    received(0, 0)
    received(0, 1)
    rest[:, 0:MAIN] = rest[:, 0:MAIN] - faces_main(halo_hot, halo[0])
    received(0, 3)
    received(0, 4)
    rest[:, 0:MAIN] = rest[:, 0:MAIN] - fringe_main(0)
    value[:, 0:MAIN] = rest[:, 0:MAIN] * inv_diag[:, 0:MAIN]
    own[1] = value[:, 0:MAIN].astype(BF16)
    for t in (0, 1):
        send_donors(1, t)
    for t in (0, 1):
        send_halo(1, t)
    received(0, 2)
    turn(halo_tail, 0)
    rest[:, MAIN:] = rest[:, MAIN:] - faces_tail(halo_tail_hot, halo_tail[0])
    received(0, 5)
    value[:, MAIN:] = (rest[:, MAIN:] - fringe_tail(0)) * inv_diag[:, MAIN:]

    stage_tail(1, 0, value[0:DONORS, MAIN:])
    send_donors(1, 2)
    stage_tail(1, 1, value[DONORS:, MAIN:])
    send_halo(1, 2)
    rest[:, 0:MAIN] = rhs_f[:, 0:MAIN] - faces_main(own_hot, own[1])
    rest[:, MAIN:] = rhs_f[:, MAIN:] - faces_tail(own_tail_hot, own_tail[1])
    rest[...] = rest[...] - applied()
    received(1, 0)
    received(1, 1)
    rest[:, 0:MAIN] = rest[:, 0:MAIN] - faces_main(halo_hot, halo[1])
    received(1, 2)
    turn(halo_tail, 1)
    rest[:, MAIN:] = rest[:, MAIN:] - faces_tail(halo_tail_hot, halo_tail[1])
    received(1, 3)
    received(1, 4)
    rest[:, 0:MAIN] = rest[:, 0:MAIN] - fringe_main(1)
    out[0:MAIN, :] = jnp.transpose(rest[:, 0:MAIN] * inv_diag[:, 0:MAIN])
    received(1, 5)
    last = (rest[:, MAIN:] - fringe_tail(1)) * inv_diag[:, MAIN:]
    out[MAIN:VALS, :] = jnp.transpose(last)[0 : VALS - MAIN, :]
    for c in range(3):
        arrived(send[c].at[sent_d if c else pl.ds(0, HALF - PART)], ds_sem.at[c])
        arrived(zpack[c].at[sent_z if c else half_rows], zs_sem.at[c])
    arrived(mid.at[half_sent], mid_sem.at[0])
    arrived(mid_pack.at[pl.ds(PART, HALF - PART)], mid_sem.at[2])
    for s in range(2):
        for n in range(6):
            arrived(moved_bytes(s, n), hs_sem.at[s, n])


def body(ckpt, rhs, npos, opos, lmat, rmat, fblk, fw, dblk, dw):
    args = (ckpt.T, rhs.T, npos.reshape(1, ROWS), opos.reshape(1, ROWS), lmat, rmat, fblk, fw, dblk, dw)
    dma = pltpu.SemaphoreType.DMA
    out = pl.pallas_call(
        kernel,
        out_shape=pltpu.VMEM((VALS, ROWS), F32),
        in_specs=[pl.BlockSpec(memory_space=pl.ANY)] * 10,
        out_specs=pl.BlockSpec(memory_space=pltpu.VMEM),
        scratch_shapes=[pltpu.VMEM(a.shape, a.dtype) for a in args]
        + [pltpu.VMEM((SLOTS, width), BF16) for _ in range(4) for width in WIDTHS]
        + [pltpu.VMEM((HALF, WIDTHS[0]), BF16)] * 2
        + [
            pltpu.VMEM((128, ROWS), F32),
            pltpu.VMEM((6 * ROWS, ROWS), BF16),
            pltpu.VMEM((6 * ROWS, DONORS), BF16),
            pltpu.VMEM((6 * ROWS, 2 * ROWS), BF16),
            pltpu.VMEM((6 * ROWS, 2 * DONORS), BF16),
            pltpu.VMEM((2 * ROWS, 3 * DONORS), BF16),
            pltpu.VMEM((2 * ROWS, 3 * 64), BF16),
            pltpu.VMEM((2, ROWS, MAIN), BF16),
            pltpu.VMEM((2, DONORS, 256), BF16),
            pltpu.VMEM((2, 2 * ROWS, MAIN), BF16),
            pltpu.VMEM((2, 2 * DONORS, 256), BF16),
            pltpu.VMEM((2, 3 * DONORS, MAIN), BF16),
            pltpu.VMEM((2, 3 * 64, 256), BF16),
            pltpu.VMEM((PADDED, 2 * PADDED), BF16),
            pltpu.VMEM((2 * PADDED, PADDED), BF16),
        ]
        + [pltpu.VMEM((6, ROWS, 128), F32)] * 3
        + [pltpu.VMEM((2, ROWS, 128), F32)] * 3
        + [pltpu.VMEM((ROWS, PADDED), F32)] * 6
        + [dma((len(args),))]
        + [dma((3,)), dma((3,)), dma((3,)), dma((3, 2)), dma((4,))]
        + [dma((2, 6))] * 2,
        compiler_params=pltpu.CompilerParams(collective_id=0, has_side_effects=True),
    )(*args)
    return out.T


def solution(mesh):
    row, vec, many = P(("blk", "grp"), None), P(("blk", "grp")), P(None, ("blk", "grp"))
    return jax.shard_map(
        body,
        mesh=mesh,
        in_specs=(row, row, vec, vec, P(), P(), many, many, many, many),
        out_specs=row,
        check_vma=False,
    )
```
